512 devices in a mesh: sec: 4 (over x), seq: 64 (over z, y), tp: 2 (over core).
Axes of the slice: x: 4, y: 8, z: 8, core: 2. Of those that a mesh axis runs over, the one named last changes fastest.
Arguments:
- hidden: bfloat16 [16384, 5120], P('seq', ('sec', 'tp')), may hold values from -6 to 6
- projection: bfloat16 [5120, 5120], P('seq', ('sec', 'tp')), may hold values from -0.078125 to 0.078125
- norm_gain: float32 [5120], replicated, may hold values from 0.1 to 1.9
- old_logp: float32 [16384], P('seq'), may hold values from -2.5 to 0
- ref_logp: float32 [16384], P('seq'), may hold values from -2.5 to 0
- lengths: int32 [256], P('seq'), may hold values from 1 to 64, 8192 in all
- group_of: int32 [256], P('seq'), may hold values from 0 to 31, as said below
- rewards: int32 [256], P('seq'), may hold values from 0 to 4
Outputs:
- ref_states: bfloat16 [8192, 5120], P('seq', ('sec', 'tp'))
- token_terms: bfloat16 [8192, 2], P('seq')
The draws below stay inside these ranges and needn't reach their ends.
Inputs may be any that keep to these rules, and one draw needn't show every extreme that they name: `group_of`: each group number names exactly 8 responses. The lengths sum to 8192; the longest is exactly 64.
All inputs are finite; a program needn't handle non-finite values. No bound on the sum of `lengths` on one device may be relied on, other than what follows from the above.
Results may differ from the reference program's by a relative error of at most 0.0039.
Values may be sent and summed in bfloat16 or wider, within the bound.
A program may use at most 64 MiB of HBM per device.

```python
import math
import jax
import jax.numpy as jnp
import numpy as np
from jax import lax

D = 5120
TOK_DEV = 128
GROUP = 8
LMAX = 64
TILE = 4
RESPONSES = 256
TOKENS = 8192
N_SEQ = 64


def draw_group_of(key, part):
    order = jax.random.permutation(key, RESPONSES)
    return (order // GROUP).astype(jnp.int32)


def touch_ends(drawn, own_key, smallest, top_value):
    shape = drawn.shape
    place = [jax.random.randint(jax.random.fold_in(own_key, axis), (), 0, shape[axis]) for axis in range(len(shape))]
    drawn = drawn.at[tuple(place)].set(smallest)
    longest = shape.index(max(shape))
    place[longest] = (place[longest] + 1) % shape[longest]
    return drawn.at[tuple(place)].set(top_value)


def levels(key, dims, split, smallest, top_value):
    gain, own = 1.0, jax.random.fold_in(key, 6)
    for position, shards_of in split:
        draws = jnp.exp(jax.random.uniform(jax.random.fold_in(own, position), (shards_of,), jnp.float32, smallest / len(split), top_value / len(split)))
        gain = gain * jnp.repeat(draws, dims[position] // shards_of).reshape([-1 if axis == position else 1 for axis in range(len(dims))])
    return gain


def profile(number_of, total, bound, lean):
    portions = [(1 << 20) // math.isqrt(standing ** lean) + 1 for standing in range(2, number_of + 1)]
    spare, given = total - bound - (number_of - 1), [1] * (number_of - 1)
    while spare > 0:
        free = [i for i in range(number_of - 1) if given[i] < bound]
        mass, left = sum([portions[i] for i in free]), spare
        for i in free:
            more = min(bound - given[i], max(1, left * portions[i] // mass), spare)
            given[i] = given[i] + more
            spare = spare - more
    return np.array([bound] + given)


def uneven_parts(stream_key, count, total, limit, lean):
    if count == 2:
        one = jax.random.randint(stream_key, (), max(1, total - limit), min(limit, total - 1) + 1)
        return jnp.stack([one, total - one])
    sizes = jnp.asarray(profile(count, total, limit, lean), jnp.int32)
    pairs = (count - 1) // 2
    source_of, receiver = sizes[1:1 + 2 * pairs:2], sizes[2:2 + 2 * pairs:2]
    margin = jnp.minimum(source_of - 1, limit - receiver)
    moved = jax.random.randint(jax.random.fold_in(stream_key, 1), (pairs,), 0, 1 << 20) % (margin + 1)
    sizes = sizes.at[1:1 + 2 * pairs:2].set(source_of - moved).at[2:2 + 2 * pairs:2].set(receiver + moved)
    return sizes[jax.random.permutation(jax.random.fold_in(stream_key, 2), count)]


def gaussian(own_key, extent, width, reach, cuts=(), kind=jnp.bfloat16):
    entries = jax.random.normal(own_key, extent, jnp.float32) * width
    if len(cuts) > 0:
        entries = levels(own_key, extent, cuts, -0.22, 0.18) * entries
    return jnp.clip(entries, min=-reach, max=reach).astype(kind)


def setup_inputs(seed: int = 0) -> dict:
    arg_keys = jax.random.split(jax.random.key(seed), 9)
    return {
        "hidden": gaussian(arg_keys[0], (RESPONSES * LMAX, D), 1.0, 6.0, ((0, 64), (1, 8))),
        "projection": gaussian(arg_keys[1], (D, D), D ** -0.5, 0.078125, ((0, 64), (1, 8))),
        "norm_gain": jnp.clip(1.0 + 0.18 * jax.random.normal(arg_keys[2], (D,), jnp.float32), 0.1, 1.9),
        "old_logp": jnp.clip(-2.5 + 2.5 * jax.random.uniform(arg_keys[3], (RESPONSES * LMAX,), jnp.float32) ** levels(arg_keys[3], (RESPONSES * LMAX,), ((0, 64),), -0.2, 0.2), -2.5, 0.0),
        "ref_logp": jnp.clip(-2.5 + 2.5 * jax.random.uniform(arg_keys[4], (RESPONSES * LMAX,), jnp.float32) ** levels(arg_keys[4], (RESPONSES * LMAX,), ((0, 64),), -0.2, 0.2), -2.5, 0.0),
        "lengths": uneven_parts(arg_keys[5], RESPONSES, TOKENS, LMAX, 2).astype(jnp.int32),
        "group_of": draw_group_of(jax.random.fold_in(arg_keys[8], 71), 0),
        "rewards": touch_ends(jax.random.randint(arg_keys[7], (RESPONSES,), 0, 5), jax.random.fold_in(arg_keys[7], 1), 0, 4).astype(jnp.int32),
    }


def refine_block(block_rows, projection, norm_gain):
    widened = block_rows.astype(jnp.float32)
    squares = lax.optimization_barrier(jnp.sum(widened * widened, axis=1, keepdims=True))
    normed = (widened * lax.rsqrt(squares / D + 1e-06) * norm_gain).astype(jnp.bfloat16)
    mixing = jnp.dot(normed, projection, preferred_element_type=jnp.float32)
    return (widened + mixing).astype(jnp.bfloat16)

def reference(hidden, projection, norm_gain, old_logp, ref_logp, lengths, group_of, rewards):
    finish = jnp.cumsum(lengths).astype(jnp.int32)
    opening = (finish - lengths).astype(jnp.int32)
    learner_row = jnp.arange(TOKENS, dtype=jnp.int32)
    shard_of = learner_row // TOK_DEV
    within = learner_row % TOK_DEV
    packed = within // TILE * (TILE * N_SEQ) + shard_of * TILE + within % TILE
    response = jnp.searchsorted(finish, packed, side='right').astype(jnp.int32)
    source = (response * LMAX + packed - jnp.take(opening, response)).astype(jnp.int32)
    gathered = jnp.take(hidden, source, axis=0)
    step_rows = math.gcd(TOKENS, 512)
    blocks = gathered.reshape(TOKENS // step_rows, step_rows, D)
    ref_states = lax.map(lambda block_rows: refine_block(block_rows, projection, norm_gain), blocks).reshape(TOKENS, D)
    member_table = (group_of[:, None] == jnp.arange(RESPONSES // GROUP, dtype=jnp.int32)[None, :]).astype(jnp.float32)
    reward_value = rewards.astype(jnp.float32)
    group_total = jnp.dot(reward_value, member_table, precision=lax.Precision.HIGHEST)
    group_square = jnp.dot(reward_value * reward_value, member_table, precision=lax.Precision.HIGHEST)
    group_mean = group_total / GROUP
    spread = jnp.maximum(jnp.sqrt(group_square / GROUP - group_mean * group_mean), 1.0)
    advantage = (reward_value - jnp.dot(member_table, group_mean, precision=lax.Precision.HIGHEST)) / jnp.dot(member_table, spread, precision=lax.Precision.HIGHEST)
    log_ratio = jnp.take(ref_logp, source) - jnp.take(old_logp, source)
    penalty = jnp.exp(log_ratio) - log_ratio - 1.0
    token_terms = jnp.stack([jnp.take(advantage, response), penalty], axis=1).astype(jnp.bfloat16)
    return (ref_states, token_terms)
```

```python
import jax
import jax.numpy as jnp
from jax import lax
from jax.experimental import pallas as pl
from jax.experimental.pallas import tpu as pltpu
from jax.sharding import PartitionSpec as P

D = 5120
GROUP = 8
LMAX = 64
COLS = 640
WROWS = 80
NX, NY, NZ = 4, 8, 8
NQ = NZ // 2
TOK = 128
SLOTS = 256
TERMS = 128
WIDE = COLS + TERMS
CUT = 384
F32 = jnp.float32
BF16 = jnp.bfloat16
MESH = pl.DeviceIdType.MESH


def iota(shape, dim):
    return lax.broadcasted_iota(jnp.int32, shape, dim)


def one_hot(mask):
    return jnp.where(mask, 1.0, 0.0).astype(BF16)


def picked(table, rows):
    return jnp.dot(table, rows, preferred_element_type=F32).astype(BF16)


def kernel(
    hidden,
    shard,
    gain,
    old_logp,
    ref_logp,
    lengths,
    group_of,
    rewards,
    states_out,
    terms_out,
    info_own,
    info_y,
    info_line,
    info_z,
    send1,
    recv1,
    send2,
    recv2,
    full_rows,
    term_pair,
    weights,
    scaled,
    product,
    give,
    take,
    squares_own,
    squares_other,
    info_ys,
    info_yr,
    info_zs,
    info_zr,
    del_s,
    del_r,
    a1_s,
    a1_r,
    a2_s,
    a2_r,
    b1_s,
    b1_r,
    b2_s,
    b2_r,
    x_s,
    x_r,
    c_s,
    c_r,
    o_s,
    o_r,
):
    x = lax.axis_index("sec")
    s = lax.axis_index("seq")
    core = lax.axis_index("tp")
    y = s % NY
    z = s // NY
    half = z % 2
    q = z // 2
    other = 1 - core

    def at(x_=None, y_=None, z_=None, core_=None):
        zz = z if z_ is None else z_
        yy = y if y_ is None else y_
        return {
            "sec": x if x_ is None else x_,
            "seq": zz * NY + yy,
            "tp": core if core_ is None else core_,
        }

    pending = []

    def remote(src, dst, ssem, rsem, dev):
        return pltpu.make_async_remote_copy(
            src_ref=src, dst_ref=dst, send_sem=ssem, recv_sem=rsem, device_id=dev, device_id_type=MESH
        )

    def send(src, dst, ssem, rsem, dev):
        copy = remote(src, dst, ssem, rsem, dev)
        copy.start()
        pending.append(copy)

    def arrived(dst, ssem, rsem):
        remote(dst, dst, ssem, rsem, at(core_=other)).wait_recv()

    barrier = pltpu.get_barrier_semaphore()
    partners = [at(y_=(y + k) % NY) for k in range(1, NY)]
    partners += [at(z_=(z + k) % NZ) for k in range(1, NZ)]
    partners += [at(z_=(z + k) % NZ, core_=other) for k in range(NZ)]
    partners += [at(x_=(x + k) % NX) for k in range(1, NX)]
    for dev in partners:
        pl.semaphore_signal(barrier, inc=1, device_id=dev, device_id_type=MESH)

    lane = iota((8, 128), 1)
    length = [lengths[i] for i in range(4)]
    group = [group_of[i] for i in range(4)]
    reward = [rewards[i].astype(F32) for i in range(4)]
    opening = [0 * length[0]]
    for i in range(3):
        opening.append(opening[-1] + length[i])
    own_total = opening[3] + length[3]
    info = jnp.where(lane == s, own_total.astype(F32), 0.0)
    for i in range(4):
        info += jnp.where(lane == 64 + group[i], reward[i], 0.0)
        info += jnp.where(lane == 96 + group[i], reward[i] * reward[i], 0.0)
    info_own[...] = info
    w_rows = pl.ds(pl.multiple_of(y * WROWS, 16), WROWS)
    weights[q, w_rows, :] = shard[...]

    pl.semaphore_wait(barrier, len(partners))

    def wrow(yy):
        return pl.ds(pl.multiple_of(yy * WROWS, 16), WROWS)

    def wa(qq, yy):
        return weights.at[qq, wrow(yy), pl.ds(0, CUT)]

    def wb(qq, yy):
        return weights.at[qq, wrow(yy), pl.ds(CUT, COLS - CUT)]

    y_up, y_dn = at(y_=(y + 1) % NY), at(y_=(y + NY - 1) % NY)
    z_up, z_dn = at(z_=(z + 2) % NZ), at(z_=(z + NZ - 2) % NZ)

    for k in range(1, NY):
        send(info_own, info_y.at[k], info_ys.at[k], info_yr.at[k], at(y_=(y + k) % NY))

    own_a = shard.at[:, pl.ds(0, CUT)]
    own_b = shard.at[:, pl.ds(CUT, COLS - CUT)]
    for k in (1, 3, 2):
        send(own_a, wa(q, y), a1_s.at[k], a1_r.at[k], at(z_=(z + 2 * k) % NZ))
    send(own_a, wa(q, y), a2_s.at[0, 1, 0], a2_r.at[0, 1, 0], y_up)
    send(own_a, wa(q, y), a2_s.at[1, 1, 0], a2_r.at[1, 1, 0], y_dn)
    for k in (1, 7, 2, 6, 3, 5, 4):
        send(own_b, wb(q, y), b1_s.at[k], b1_r.at[k], at(y_=(y + k) % NY))
    send(own_b, wb(q, y), b2_s.at[0, 1, 0], b2_r.at[0, 1, 0], z_up)
    send(own_b, wb(q, y), b2_s.at[1, 1, 0], b2_r.at[1, 1, 0], z_dn)

    line = info
    for k in range(1, NY):
        arrived(info_y.at[k], info_ys.at[k], info_yr.at[k])
        line += info_y[k]
    info_line[...] = line
    for k in range(1, NZ):
        send(info_line, info_z.at[k], info_zs.at[k], info_zr.at[k], at(z_=(z + k) % NZ))

    for k in (1, 3, 2):
        qq = (q + NQ - k) % NQ
        piece = wa(qq, y)
        arrived(piece, a1_s.at[k], a1_r.at[k])
        j = NQ - k
        send(piece, piece, a2_s.at[0, 1, j], a2_r.at[0, 1, j], y_up)
        send(piece, piece, a2_s.at[1, 1, j], a2_r.at[1, 1, j], y_dn)
    for k in (1, 7, 2, 6, 3, 5, 4):
        yy = (y + NY - k) % NY
        piece = wb(q, yy)
        arrived(piece, b1_s.at[k], b1_r.at[k])
        j = NY - k
        send(piece, piece, b2_s.at[0, 1, j], b2_r.at[0, 1, j], z_up)
        send(piece, piece, b2_s.at[1, 1, j], b2_r.at[1, 1, j], z_dn)

    def forward_a(d):
        for j in (0, 3, 1, 2):
            qq = (q + j) % NQ
            for way, dev in ((0, y_up), (1, y_dn)):
                if d == 4 and (j < 2) != (way == 0):
                    continue
                yy = (y + NY - d) % NY if way == 0 else (y + d) % NY
                piece = wa(qq, yy)
                arrived(piece, a2_s.at[way, d, j], a2_r.at[way, d, j])
                if d < 3 or (d == 3 and (j < 2) == (way == 0)):
                    send(piece, piece, a2_s.at[way, d + 1, j], a2_r.at[way, d + 1, j], dev)

    def forward_b(d):
        for j in (0, 7, 1, 6, 2, 5, 3, 4):
            yy = (y + j) % NY
            for way, dev in ((0, z_up), (1, z_dn)):
                mine = (j < 4) == (way == 0)
                if d == 2 and not mine:
                    continue
                qq = (q + NQ - d) % NQ if way == 0 else (q + d) % NQ
                piece = wb(qq, yy)
                arrived(piece, b2_s.at[way, d, j], b2_r.at[way, d, j])
                if d == 1 and mine:
                    send(piece, piece, b2_s.at[way, 2, j], b2_r.at[way, 2, j], dev)

    total = line
    for k in range(1, NZ):
        arrived(info_z.at[k], info_zs.at[k], info_zr.at[k])
        total += info_z[k]

    first = (jnp.sum(jnp.where(lane < s, total, 0.0)) * 0.125).astype(jnp.int32)
    col = iota((1, SLOTS), 1)
    spot = jnp.full((1, SLOTS), -1, jnp.int32)
    for i in range(4):
        p = col - i * LMAX
        spot = jnp.where((p >= 0) & (p < length[i]), opening[i] + p, spot)
    row = iota((SLOTS, 1), 0)
    turned = ((row // 4 % 8) * 8 + row // 32) * 4 + row % 4
    table1 = one_hot((((turned - first) & (SLOTS - 1))) == spot)
    table2 = one_hot((((row - first) & (SLOTS - 1))) == spot)

    mean = total * (1.0 / GROUP)
    mean_square = pltpu.roll(mean, 96, 1)
    spread = jnp.maximum(jnp.sqrt(mean_square - mean * mean), 1.0)
    adv_col = jnp.zeros((SLOTS, 1), F32)
    for i in range(4):
        value = jnp.where(lane == 64 + group[i], (reward[i] - mean) / spread, 0.0)
        adv_col = jnp.where(row // LMAX == i, jnp.sum(value) * 0.125, adv_col)
    ratio = ref_logp[...] - old_logp[...]
    penalty = jnp.exp(ratio) - ratio - 1.0
    pen_col = jnp.sum(jnp.where(row == col, penalty, 0.0), axis=1, keepdims=True)
    term_lane = iota((SLOTS, TERMS), 1)
    terms = jnp.where(term_lane == 0, adv_col, jnp.where(term_lane == 1, pen_col, 0.0)).astype(BF16)

    send1[:, :CUT] = picked(table1, hidden[:, :CUT])
    send1[:, CUT:COLS] = picked(table2, hidden[:, CUT:])
    send1[:, COLS:] = picked(table2, terms)

    lanes1, lanes2 = pl.ds(0, CUT), pl.ds(CUT, WIDE - CUT)
    zme = 2 * q + core
    aligned = half == core

    def block(i):
        return pl.ds(pl.multiple_of(i * 32, 32), 32)

    def route_y(n, src, dst, lanes):
        dst[block(y), lanes] = src[block(y), lanes]
        for k in (4, 3, 5, 2, 6, 1, 7):
            t = (y + k) % NY
            send(src.at[block(t), lanes], dst.at[block(y), lanes], del_s.at[n, k], del_r.at[n, k], at(y_=t))

    def wait_y(n, dst, lanes):
        for k in range(1, NY):
            arrived(dst.at[block((y + NY - k) % NY), lanes], del_s.at[n, k], del_r.at[n, k])

    def z_target(zt):
        return at(z_=2 * (zt // 2) + core, core_=zt % 2)

    def route_z(n, src, dst, lanes):
        for k in (4, 3, 5, 2, 6, 1, 7):
            zt = (z + k) % NZ
            send(src.at[block(zt), lanes], dst.at[block(z), lanes], del_s.at[n, k], del_r.at[n, k], z_target(zt))

        @pl.when(aligned)
        def _():
            dst[block(z), lanes] = src[block(z), lanes]

        @pl.when(jnp.logical_not(aligned))
        def _():
            remote(
                src.at[block(z), lanes], dst.at[block(z), lanes], del_s.at[n, 0], del_r.at[n, 0],
                at(z_=2 * q + core, core_=other),
            ).start()

    def wait_z(n, dst, lanes):
        for k in range(1, NZ):
            arrived(dst.at[block((zme + NZ - k) % NZ), lanes], del_s.at[n, k], del_r.at[n, k])

        @pl.when(jnp.logical_not(aligned))
        def _():
            arrived(dst.at[block(zme), lanes], del_s.at[n, 0], del_r.at[n, 0])

    def sent_z(n, src, lanes):
        @pl.when(jnp.logical_not(aligned))
        def _():
            remote(
                src.at[block(z), lanes], src.at[block(z), lanes], del_s.at[n, 0], del_r.at[n, 0],
                at(z_=2 * q + core, core_=other),
            ).wait_send()

    route_y(0, send1, recv1, lanes1)
    route_z(1, send1, recv1, lanes2)

    forward_a(1)

    wait_y(0, recv1, lanes1)
    wait_z(1, recv1, lanes2)
    inner = iota((1, SLOTS), 1)
    swap = one_hot(((row // 4 % 8) * 8 + row // 32) * 4 + row % 4 == inner)
    send2[...] = picked(swap, recv1[...])
    route_z(2, send2, recv2, lanes1)
    route_y(3, send2, recv2, lanes2)

    forward_b(1)
    forward_a(2)

    counts = total.astype(BF16)
    sender = iota((128, SLOTS), 0)
    slot = iota((128, SLOTS), 1)
    natural = slot // 4
    swapped = (natural % 8) * 8 + natural // 8
    w = iota((TOK, 1), 0)
    packed = ((w // 4) * SLOTS + (zme * NY + y) * 4 + w % 4).astype(F32)
    same = w % 4 == col % 4

    def pick_table(order):
        low = jnp.dot(counts, one_hot(sender < order), preferred_element_type=F32)[0:1]
        high = jnp.dot(counts, one_hot(sender <= order), preferred_element_type=F32)[0:1]
        return one_hot((low <= packed) & (packed < high) & same)

    pick1, pick2 = pick_table(natural), pick_table(swapped)

    wait_z(2, recv2, lanes1)
    wait_y(3, recv2, lanes2)
    mine = pl.multiple_of(core * TOK, TOK)
    theirs = pl.multiple_of(other * TOK, TOK)
    full_rows[x, pl.ds(mine, TOK), :CUT] = picked(pick1, recv2[:, :CUT])
    full_rows[x, pl.ds(mine, TOK), CUT:] = picked(pick2, recv2[:, CUT:COLS])
    term_pair[core] = picked(pick2, recv2[:, COLS:])

    H = TOK // 2
    x_up, x_dn = at(x_=(x + 1) % NX), at(x_=(x + NX - 1) % NX)
    mate = at(core_=other)
    x_l, x_r1, x_f = (x + NX - 1) % NX, (x + 1) % NX, (x + 2) % NX

    def part(xx, base, i):
        return full_rows.at[xx, pl.ds(pl.multiple_of(base + i * H, H), H), :]

    def whole(xx, base):
        return full_rows.at[xx, pl.ds(base, TOK), :]

    send(part(x, mine, 0), part(x, mine, 0), x_s.at[0, 0], x_r.at[0, 0], x_up)
    send(part(x, mine, 1), part(x, mine, 1), x_s.at[1, 1], x_r.at[1, 1], x_dn)
    send(part(x, mine, 1), part(x, mine, 1), x_s.at[0, 1], x_r.at[0, 1], x_up)
    send(part(x, mine, 0), part(x, mine, 0), x_s.at[1, 0], x_r.at[1, 0], x_dn)
    send(whole(x, mine), whole(x, mine), c_s.at[0], c_r.at[0], mate)
    send(term_pair.at[core], term_pair.at[core], c_s.at[4], c_r.at[4], mate)

    forward_a(3)

    arrived(part(x_l, mine, 0), x_s.at[0, 0], x_r.at[0, 0])
    send(part(x_l, mine, 0), part(x_l, mine, 0), x_s.at[0, 2], x_r.at[0, 2], x_up)
    arrived(part(x_r1, mine, 1), x_s.at[1, 1], x_r.at[1, 1])
    send(part(x_r1, mine, 1), part(x_r1, mine, 1), x_s.at[1, 2], x_r.at[1, 2], x_dn)
    arrived(part(x_l, mine, 1), x_s.at[0, 1], x_r.at[0, 1])
    send(whole(x_l, mine), whole(x_l, mine), c_s.at[1], c_r.at[1], mate)
    arrived(part(x_r1, mine, 0), x_s.at[1, 0], x_r.at[1, 0])
    send(whole(x_r1, mine), whole(x_r1, mine), c_s.at[2], c_r.at[2], mate)
    arrived(part(x_f, mine, 0), x_s.at[0, 2], x_r.at[0, 2])
    arrived(part(x_f, mine, 1), x_s.at[1, 2], x_r.at[1, 2])
    send(whole(x_f, mine), whole(x_f, mine), c_s.at[3], c_r.at[3], mate)

    square = jnp.zeros((2 * TOK, 128), F32)
    for n, xx in enumerate((x, x_l, x_r1, x_f)):
        arrived(whole(xx, theirs), c_s.at[n], c_r.at[n])
        wide = full_rows[xx].astype(F32)
        g = gain[:, pl.ds(pl.multiple_of((2 * xx + half) * COLS, 128), COLS)]
        scaled[xx] = (wide * g).astype(BF16)
        for t in range(COLS // 128):
            tile = wide[:, t * 128 : (t + 1) * 128]
            square += tile * tile
    squares_own[...] = lax.dot_general(
        jnp.ones((8, 128), F32), square, (((1,), (1,)), ((), ())),
        precision=lax.Precision.HIGHEST, preferred_element_type=F32,
    )
    z_mate = at(z_=z + 1 - 2 * half)
    send(squares_own, squares_other, o_s.at[0], o_r.at[0], z_mate)
    arrived(term_pair.at[other], c_s.at[4], c_r.at[4])
    terms_out[...] = term_pair[half][:, :2]

    forward_a(4)
    for lanes in (pl.ds(0, CUT), pl.ds(CUT, COLS - CUT)):
        if lanes.start == CUT:
            forward_b(2)
        acc = jnp.dot(scaled[0], weights[0, :, lanes], preferred_element_type=F32)
        for i in range(1, NX):
            acc += jnp.dot(scaled[i], weights[i, :, lanes], preferred_element_type=F32)
        product[:, lanes] = acc

    arrived(squares_other, o_s.at[0], o_r.at[0])
    both = (squares_own[...] + squares_other[...])[0:1]
    rate = lax.rsqrt(both * (1.0 / D) + 1e-6)
    scale = jnp.sum(jnp.where(row == col, rate, 0.0), axis=1, keepdims=True)
    kept = jnp.where(aligned, 1.0, 0.0)
    refined = product[...] * scale + full_rows[x].astype(F32) * kept
    product[...] = refined
    away = pl.multiple_of((1 - half) * TOK, TOK)
    home = pl.multiple_of(half * TOK, TOK)
    give[...] = product[pl.ds(away, TOK), :].astype(BF16)
    send(give, take, o_s.at[1], o_r.at[1], z_mate)
    arrived(take, o_s.at[1], o_r.at[1])
    states_out[...] = (product[pl.ds(home, TOK), :] + take[...].astype(F32)).astype(BF16)

    for copy in pending:
        copy.wait_send()
    sent_z(1, send1, lanes2)
    sent_z(2, send2, lanes1)


def shards(hidden, projection, norm_gain, old_logp, ref_logp, lengths, group_of, rewards):
    dma = pltpu.SemaphoreType.DMA
    vmem = pl.BlockSpec(memory_space=pltpu.VMEM)
    smem = pl.BlockSpec(memory_space=pltpu.SMEM)
    pairs = []
    for shape in ((8,), (8,), (4, 8), (4,), (2, 5, 4), (8,), (2, 3, 8), (2, 3), (5,), (2,)):
        pairs += [dma(shape), dma(shape)]
    return pl.pallas_call(
        kernel,
        out_shape=(
            jax.ShapeDtypeStruct((TOK, COLS), BF16),
            jax.ShapeDtypeStruct((TOK, 2), BF16),
        ),
        in_specs=[vmem] * 5 + [smem] * 3,
        out_specs=(vmem, vmem),
        scratch_shapes=[
            pltpu.VMEM((8, 128), F32),
            pltpu.VMEM((NY, 8, 128), F32),
            pltpu.VMEM((8, 128), F32),
            pltpu.VMEM((NZ, 8, 128), F32),
            pltpu.VMEM((SLOTS, WIDE), BF16),
            pltpu.VMEM((SLOTS, WIDE), BF16),
            pltpu.VMEM((SLOTS, WIDE), BF16),
            pltpu.VMEM((SLOTS, WIDE), BF16),
            pltpu.VMEM((NX, 2 * TOK, COLS), BF16),
            pltpu.VMEM((2, TOK, TERMS), BF16),
            pltpu.VMEM((NQ, COLS, COLS), BF16),
            pltpu.VMEM((NX, 2 * TOK, COLS), BF16),
            pltpu.VMEM((2 * TOK, COLS), F32),
            pltpu.VMEM((TOK, COLS), BF16),
            pltpu.VMEM((TOK, COLS), BF16),
            pltpu.VMEM((8, 2 * TOK), F32),
            pltpu.VMEM((8, 2 * TOK), F32),
        ]
        + pairs,
        compiler_params=pltpu.CompilerParams(collective_id=0, has_side_effects=True),
    )(
        hidden,
        projection,
        norm_gain.reshape(1, D),
        old_logp.reshape(1, SLOTS),
        ref_logp.reshape(1, SLOTS),
        lengths,
        group_of,
        rewards,
    )


def solution(mesh):
    in_specs = (
        P("seq", ("sec", "tp")),
        P("seq", ("sec", "tp")),
        P(),
        P("seq"),
        P("seq"),
        P("seq"),
        P("seq"),
        P("seq"),
    )
    out_specs = (P("seq", ("sec", "tp")), P("seq", None))
    return jax.shard_map(shards, mesh=mesh, in_specs=in_specs, out_specs=out_specs, check_vma=False)
```

```python
import jax
import jax.numpy as jnp
from jax import lax
from jax.experimental import pallas as pl
from jax.experimental.pallas import tpu as pltpu
from jax.sharding import PartitionSpec as P

D = 5120
GROUP = 8
LMAX = 64
COLS = 640
BOTH = 2 * COLS
WROWS = 80
NX, NY, NZ = 4, 8, 8
NQ = NZ // 2
TOK = 128
SLOTS = 256
TERMS = 128
CUT = 384
WIDE = COLS + TERMS
WCUT = 768
F32 = jnp.float32
BF16 = jnp.bfloat16
MESH = pl.DeviceIdType.MESH
ORDER = (
    (2, 0, 1), (2, 1, 1), (3, 1, 0, 0), (3, 1, 1, 0), (0, 0), (0, 1), (2, 0, 2), (2, 1, 2),
    (4, 1, 0, 0), (3, 2, 0, 0), (3, 2, 1, 0), (3, 1, 0, 3), (3, 1, 1, 3), (4, 1, 1, 7), (3, 1, 0, 1), (3, 1, 1, 1),
    (4, 1, 0, 1), (2, 0, 3), (2, 1, 3), (1, 0), (1, 1), (3, 3, 0, 0), (3, 2, 0, 3), (3, 2, 1, 3),
    (4, 1, 1, 6), (3, 2, 0, 1), (3, 2, 1, 1), (2, 0, 4), (2, 1, 4), (4, 1, 0, 2), (3, 1, 0, 2), (3, 1, 1, 2),
    (3, 3, 1, 3), (4, 1, 1, 5), (3, 3, 0, 1), (3, 2, 1, 2), (3, 2, 0, 2), (4, 1, 0, 3), (3, 3, 1, 2), (4, 1, 1, 4),
)


def iota(shape, dim):
    return lax.broadcasted_iota(jnp.int32, shape, dim)


def one_hot(mask):
    return jnp.where(mask, 1.0, 0.0).astype(BF16)


def picked(table, rows):
    return jnp.dot(table, rows, preferred_element_type=F32).astype(BF16)


def flat(rows):
    return rows.reshape(SLOTS, rows.shape[-1])


def tiles(rows):
    return rows.reshape(8, 32, rows.shape[-1])


class Links:
    def __init__(self):
        self.x, self.s, self.core = (lax.axis_index(n) for n in ("sec", "seq", "tp"))
        self.y, self.z = self.s % NY, self.s // NY
        self.half, self.q = self.z % 2, self.z // 2
        self.pending = []

    def at(self, x=None, y=None, z=None, core=None):
        zz = self.z if z is None else z
        yy = self.y if y is None else y
        return {
            "sec": self.x if x is None else x,
            "seq": zz * NY + yy,
            "tp": self.core if core is None else core,
        }

    def remote(self, src, dst, sems, dev):
        return pltpu.make_async_remote_copy(
            src_ref=src, dst_ref=dst, send_sem=sems[0], recv_sem=sems[1], device_id=dev, device_id_type=MESH
        )

    def send(self, src, dst, sems, dev):
        copy = self.remote(src, dst, sems, dev)
        copy.start()
        self.pending.append(copy)

    def arrived(self, dst, sems):
        self.remote(dst, dst, sems, self.at(core=1 - self.core)).wait_recv()

    def finish(self):
        for copy in self.pending:
            copy.wait_send()


def pair(sems, *index):
    return sems[0].at[index], sems[1].at[index]


def product_core(net, refs, sems):
    shard, gain, weights, scaled, raw, product, give, take, home, squares, hidden, hidden0, terms, states_out, terms_out = refs
    swap_sem, pa, pf, pb, a2, b2, r_sem, o_sem, own_sem = sems
    x, y, z, q, half = net.x, net.y, net.z, net.q, net.half
    zm = z + 1 - 2 * half
    mate = net.at(core=1)

    def rows(qq, yy):
        return pl.ds(pl.multiple_of(qq * COLS + yy * WROWS, 16), WROWS)

    def wa(qq, yy):
        return weights.at[rows(qq, yy), pl.ds(0, WCUT)]

    def wb(qq, yy):
        return weights.at[rows(qq, yy), pl.ds(WCUT, BOTH - WCUT)]

    def wa_part(qq, yy, way):
        return weights.at[rows(qq, yy), pl.ds(way * WCUT // 2, WCUT // 2)]

    def wb_part(qq, yy, way):
        return weights.at[rows(qq, yy), pl.ds(WCUT + way * (BOTH - WCUT) // 2, (BOTH - WCUT) // 2)]

    y_way = net.at(y=(y + 1) % NY), net.at(y=(y + NY - 1) % NY)
    z_way = net.at(z=(z + 2) % NZ), net.at(z=(z + NZ - 2) % NZ)

    def along_y(j):
        piece = wa((q + j) % NQ, y)
        for way in (0, 1):
            net.send(piece, piece, pair(a2, way, 1, j), y_way[way])

    def along_z(j):
        piece = wb(q, (y + j) % NY)
        for way in (0, 1):
            net.send(piece, piece, pair(b2, way, 1, j), z_way[way])

    own = pltpu.make_async_copy(shard, weights.at[rows(q, y), pl.ds(0, COLS)], own_sem.at[0])
    own.start()
    net.send(hidden, hidden0, pair(swap_sem, 0), mate)
    own.wait()
    net.arrived(weights.at[rows(q, y), pl.ds(COLS, COLS)], pair(swap_sem, 1))
    for way in (0, 1):
        net.send(wa(q, y), wa(q, y), pair(pa, way), z_way[way])
    for way in (0, 1):
        net.send(wb(q, y), wb(q, y), pair(pb, way, 1), y_way[way])
    along_y(0)
    along_z(0)

    met = []

    def first_a(way):
        qq = (q + 3 - 2 * way) % NQ
        net.arrived(wa(qq, y), pair(pa, way))
        part = wa_part(qq, y, way)
        net.send(part, part, pair(pf, way), z_way[way])
        along_y(3 - 2 * way)

    def far_a(way):
        net.arrived(wa_part((q + 2) % NQ, y, way), pair(pf, way))
        if "far" in met:
            along_y(2)
        met.append("far")

    def first_b(way, d):
        yy = (y + (d if way else NY - d)) % NY
        part = wb_part(q, yy, way)
        piece = part if d == 4 else wb(q, yy)
        net.arrived(piece, pair(pb, way, d))
        if d < 3:
            net.send(piece, piece, pair(pb, way, d + 1), y_way[way])
        elif d == 3:
            net.send(part, part, pair(pb, way, 4), y_way[way])
        if d < 4:
            along_z(d if way else NY - d)
        elif "half" in met:
            along_z(4)
        else:
            met.append("half")

    waiting = [(3, d, way, j) for d in (1, 2, 3) for way in (0, 1) for j in range(NQ)]
    waiting += [(3, 4, j // 2, j) for j in range(NQ)]
    waiting += [(4, 1, way, j) for way in (0, 1) for j in range(NY)]
    waiting += [(4, 2, j // 4, j) for j in range(NY)]

    def next_a(d, way, j):
        waiting.remove((3, d, way, j))
        piece = wa((q + j) % NQ, (y + (d if way else NY - d)) % NY)
        net.arrived(piece, pair(a2, way, d, j))
        if d < 3 or (d == 3 and j // 2 == way):
            net.send(piece, piece, pair(a2, way, d + 1, j), y_way[way])

    def next_b(d, way, j):
        waiting.remove((4, d, way, j))
        piece = wb((q + (d if way else NQ - d)) % NQ, (y + j) % NY)
        net.arrived(piece, pair(b2, way, d, j))
        if d == 1 and j // 4 == way:
            net.send(piece, piece, pair(b2, way, 2, j), z_way[way])

    hops = (first_a, far_a, first_b, next_a, next_b)
    for kind, *index in ORDER:
        hops[kind](*index)

    for n, xx in enumerate((x, (x + NX - 1) % NX, (x + 1) % NX, (x + 2) % NX)):
        for i in range(2):
            net.arrived(raw.at[xx, pl.ds(i * TOK, TOK), :], pair(r_sem, n, i))
        g = gain[:, pl.ds(pl.multiple_of((2 * xx + half) * COLS, 128), COLS)]
        scaled[:, pl.ds(pl.multiple_of(xx * COLS, 128), COLS)] = (raw[xx].astype(F32) * g).astype(BF16)
    net.arrived(terms, pair(o_sem, 5))
    terms_out[...] = terms[:, :2]
    net.arrived(squares.at[0], pair(o_sem, 0))
    net.arrived(squares.at[1], pair(o_sem, 1))
    rate = lax.rsqrt((squares[0] + squares[1])[0:1] * (1.0 / D) + 1e-6)
    scale = jnp.sum(jnp.where(iota((SLOTS, 1), 0) == iota((1, SLOTS), 1), rate, 0.0), axis=1, keepdims=True)
    away = pl.ds(pl.multiple_of((1 - half) * TOK, TOK), TOK)
    near = pl.ds(pl.multiple_of(half * TOK, TOK), TOK)

    for c, kind in ((0, 3), (1, 4)):
        for item in [w for w in waiting if w[0] == kind]:
            hops[kind](*item[1:])
        cols = pl.ds(c * COLS, COLS)
        part = jnp.dot(scaled[...], weights[:, cols], preferred_element_type=F32)
        kept = jnp.where(half == c, 1.0, 0.0)
        product[:, cols] = part * scale + raw[x].astype(F32) * kept
        give[c] = product[away, cols].astype(BF16)
        net.send(give.at[c], take, pair(o_sem, 2 + c), net.at(z=zm, core=c))
    net.send(product.at[near, pl.ds(COLS, COLS)], home, pair(o_sem, 4), mate)
    net.arrived(take, pair(o_sem, 2))
    states_out[...] = (product[near, :COLS] + take[...].astype(F32)).astype(BF16)
    net.finish()


def token_core(net, refs, sems):
    (
        hidden, hidden0, shard, old_logp, ref_logp, lengths, group_of, rewards, weights,
        info_own, info_y, info_line, info_z, send1, r1a, r1b, s2a, s2b, r2a, r2b,
        full_rows, terms, squares_own, squares, take, home, raw, states_out, terms_out,
    ) = refs
    swap_sem, iy, iz, del_sem, x_sem, r_sem, o_sem, own_info = sems
    x, y, z, q, half, s = net.x, net.y, net.z, net.q, net.half, net.s
    zm = z + 1 - 2 * half
    mate = net.at(core=0)
    info, length, group, reward, opening = own_info

    for k in range(1, NY):
        net.send(info_own, info_y.at[k], pair(iy, k), net.at(y=(y + k) % NY))
    own_rows = pl.ds(pl.multiple_of(q * COLS + y * WROWS, 16), WROWS)
    net.send(shard, weights.at[own_rows, pl.ds(COLS, COLS)], pair(swap_sem, 1), mate)
    line = info
    for k in range(1, NY):
        net.arrived(info_y.at[k], pair(iy, k))
        line += info_y[k]
    info_line[...] = line
    for k in range(1, NZ):
        net.send(info_line, info_z.at[k], pair(iz, k), net.at(z=(z + k) % NZ))

    lane = iota((8, 128), 1)
    col = iota((1, SLOTS), 1)
    spot = jnp.full((1, SLOTS), -1, jnp.int32)
    for i in range(4):
        p = col - i * LMAX
        spot = jnp.where((p >= 0) & (p < length[i]), opening[i] + p, spot)
    row = iota((SLOTS, 1), 0)
    turned = ((row // 4 % 8) * 8 + row // 32) * 4 + row % 4
    ratio = ref_logp[...] - old_logp[...]
    penalty = jnp.exp(ratio) - ratio - 1.0
    pen_col = jnp.sum(jnp.where(row == col, penalty, 0.0), axis=1, keepdims=True)
    swap = one_hot(turned == col)
    net.arrived(hidden0, pair(swap_sem, 0))

    total = line
    for k in range(1, NZ):
        net.arrived(info_z.at[k], pair(iz, k))
        total += info_z[k]

    first = (jnp.sum(jnp.where(lane < s, total, 0.0)) * 0.125).astype(jnp.int32)
    table1 = one_hot((((turned - first) & (SLOTS - 1))) == spot)
    table2 = one_hot((((row - first) & (SLOTS - 1))) == spot)
    lanes1, lanes2 = pl.ds(0, CUT), pl.ds(CUT, WIDE - CUT)

    def route_y(n, src, dst, lanes):
        dst[:, y] = src[:, y, :, lanes]
        for k in (4, 3, 5, 2, 6, 1, 7):
            t = (y + k) % NY
            net.send(src.at[:, t, :, lanes], dst.at[:, y], pair(del_sem, n, k), net.at(y=t))

    def wait_y(n, dst):
        for k in range(1, NY):
            net.arrived(dst.at[:, (y + NY - k) % NY], pair(del_sem, n, k))

    def route_z(n, src, dst, lanes):
        dst[z] = src[half, pl.ds(2 * q, 2), :, lanes]
        for k in (4, 3, 5, 2, 6, 1, 7):
            t = (z + k) % NZ
            net.send(src.at[t % 2, pl.ds(2 * (t // 2), 2), :, lanes], dst.at[z], pair(del_sem, n, k), net.at(z=t))

    def wait_z(n, dst):
        for k in range(1, NZ):
            net.arrived(dst.at[(z + NZ - k) % NZ], pair(del_sem, n, k))

    send1[0, :, :, :CUT] = tiles(picked(table1, hidden0[:, :CUT]))
    send1[1, :, :, :CUT] = tiles(picked(table1, hidden[:, :CUT]))
    route_y(0, send1, r1a, lanes1)

    mean = total * (1.0 / GROUP)
    mean_square = pltpu.roll(mean, 96, 1)
    spread = jnp.maximum(jnp.sqrt(mean_square - mean * mean), 1.0)
    adv_col = jnp.zeros((SLOTS, 1), F32)
    for i in range(4):
        value = jnp.where(lane == 64 + group[i], (reward[i] - mean) / spread, 0.0)
        adv_col = jnp.where(row // LMAX == i, jnp.sum(value) * 0.125, adv_col)
    term_lane = iota((SLOTS, TERMS), 1)
    own_terms = jnp.where(term_lane == 0, adv_col, jnp.where(term_lane == 1, pen_col, 0.0)).astype(BF16)
    send1[0, :, :, CUT:COLS] = tiles(picked(table2, hidden0[:, CUT:]))
    send1[1, :, :, CUT:COLS] = tiles(picked(table2, hidden[:, CUT:]))
    moved = tiles(picked(table2, own_terms))
    send1[0, :, :, COLS:] = moved
    send1[1, :, :, COLS:] = moved
    route_z(1, send1, r1b, lanes2)

    counts = total.astype(BF16)
    sender = iota((128, SLOTS), 0)
    natural = iota((128, SLOTS), 1) // 4
    swapped = (natural % 8) * 8 + natural // 8
    w = iota((TOK, 1), 0)
    same = w % 4 == col % 4

    def bounds(order):
        low = jnp.dot(counts, one_hot(sender < order), preferred_element_type=F32)[0:1]
        high = jnp.dot(counts, one_hot(sender <= order), preferred_element_type=F32)[0:1]
        return low, high

    def pick_table(limits, e):
        packed = ((w // 4) * SLOTS + ((2 * q + e) * NY + y) * 4 + w % 4).astype(F32)
        return one_hot((limits[0] <= packed) & (packed < limits[1]) & same)

    limits1, limits2 = bounds(natural), bounds(swapped)
    pick1 = [pick_table(limits1, e) for e in range(2)]
    pick2 = [pick_table(limits2, e) for e in range(2)]

    whole = pl.ds(0, CUT)
    wait_y(0, r1a)
    for c in range(2):
        s2a[c] = tiles(picked(swap, flat(r1a[c])))
    route_z(2, s2a, r2a, whole)
    wait_z(1, r1b)
    for e in range(2):
        s2b[e] = tiles(picked(swap, flat(r1b[:, e])))
    route_y(3, s2b, r2b, whole)

    wait_z(2, r2a)
    for e in range(2):
        full_rows[x, e * TOK : (e + 1) * TOK, :CUT] = picked(pick1[e], flat(r2a[:, e]))
    wait_y(3, r2b)
    for e in range(2):
        full_rows[x, e * TOK : (e + 1) * TOK, CUT:] = picked(pick2[e], flat(r2b[e, :, :, : COLS - CUT]))

    x_up, x_dn = net.at(x=(x + 1) % NX), net.at(x=(x + NX - 1) % NX)
    x_l, x_r, x_f = (x + NX - 1) % NX, (x + 1) % NX, (x + 2) % NX

    def part(xx, i):
        return full_rows.at[xx, pl.ds(i * TOK, TOK), :]

    def over(xx, i, way, slot):
        net.send(part(xx, i), part(xx, i), pair(x_sem, way, slot), (x_up, x_dn)[way])

    def down(xx, n, i):
        net.send(part(xx, i), raw.at[xx, pl.ds(i * TOK, TOK), :], pair(r_sem, n, i), mate)

    over(x, 0, 0, 0)
    over(x, 1, 1, 1)
    over(x, 1, 0, 1)
    over(x, 0, 1, 0)
    down(x, 0, 0)
    down(x, 0, 1)
    chosen = jnp.where(half == 0, pick2[0].astype(F32), pick2[1].astype(F32)).astype(BF16)
    terms[...] = picked(chosen, flat(r2b[half, :, :, COLS - CUT :]))
    net.send(terms, terms, pair(o_sem, 5), mate)
    terms_out[...] = terms[:, :2]

    square = [jnp.zeros((2 * TOK, 128), F32)]

    def add_squares(xx):
        wide = full_rows[xx].astype(F32)
        for t in range(COLS // 128):
            tile = wide[:, t * 128 : (t + 1) * 128]
            square[0] += tile * tile

    add_squares(x)
    net.arrived(part(x_l, 0), pair(x_sem, 0, 0))
    over(x_l, 0, 0, 2)
    net.arrived(part(x_r, 1), pair(x_sem, 1, 1))
    over(x_r, 1, 1, 2)
    down(x_l, 1, 0)
    down(x_r, 2, 1)
    net.arrived(part(x_l, 1), pair(x_sem, 0, 1))
    down(x_l, 1, 1)
    net.arrived(part(x_r, 0), pair(x_sem, 1, 0))
    down(x_r, 2, 0)
    add_squares(x_l)
    add_squares(x_r)
    net.arrived(part(x_f, 0), pair(x_sem, 0, 2))
    down(x_f, 3, 0)
    net.arrived(part(x_f, 1), pair(x_sem, 1, 2))
    down(x_f, 3, 1)
    add_squares(x_f)
    squares_own[...] = lax.dot_general(
        jnp.ones((8, 128), F32), square[0], (((1,), (1,)), ((), ())),
        precision=lax.Precision.HIGHEST, preferred_element_type=F32,
    )
    net.send(squares_own, squares.at[0], pair(o_sem, 0), mate)
    net.send(squares_own, squares.at[1], pair(o_sem, 1), net.at(z=zm, core=0))

    net.arrived(home, pair(o_sem, 4))
    net.arrived(take, pair(o_sem, 3))
    states_out[...] = (home[...] + take[...].astype(F32)).astype(BF16)
    net.finish()


SCRATCH = dict(
    info_own=((8, 128), F32),
    info_y=((NY, 8, 128), F32),
    info_line=((8, 128), F32),
    info_z=((NZ, 8, 128), F32),
    send1=((2, 8, 32, WIDE), BF16),
    r1a=((2, 8, 32, CUT), BF16),
    r1b=((8, 2, 32, CUT), BF16),
    s2a=((2, 8, 32, CUT), BF16),
    s2b=((2, 8, 32, CUT), BF16),
    r2a=((8, 2, 32, CUT), BF16),
    r2b=((2, 8, 32, CUT), BF16),
    full_rows=((NX, 2 * TOK, COLS), BF16),
    raw=((NX, 2 * TOK, COLS), BF16),
    terms=((TOK, TERMS), BF16),
    hidden0=((SLOTS, COLS), BF16),
    weights=((NQ * COLS, BOTH), BF16),
    scaled=((2 * TOK, NX * COLS), BF16),
    product=((2 * TOK, BOTH), F32),
    give=((2, TOK, COLS), BF16),
    take=((TOK, COLS), BF16),
    home=((TOK, COLS), F32),
    squares_own=((8, 2 * TOK), F32),
    squares=((2, 8, 2 * TOK), F32),
)
SEMAPHORES = dict(
    swap=(2,),
    iy=(8,),
    iz=(8,),
    deliver=(4, 8),
    pa=(2,),
    pf=(2,),
    pb=(2, 5),
    a2=(2, 5, 4),
    b2=(2, 3, 8),
    x=(2, 3),
    r=(4, 2),
    o=(6,),
)


def kernel(hidden, shard, gain, old_logp, ref_logp, lengths, group_of, rewards, states_out, terms_out, *rest):
    v = dict(zip(SCRATCH, rest))
    sem_refs = rest[len(SCRATCH) :]
    m = {n: (sem_refs[2 * i], sem_refs[2 * i + 1]) for i, n in enumerate(SEMAPHORES)}
    own_sem = sem_refs[-1]

    net = Links()
    y, z = net.y, net.z
    other = 1 - net.core
    barrier = pltpu.get_barrier_semaphore()
    partners = [net.at(y=(y + k) % NY) for k in range(1, NY)]
    partners += [net.at(z=(z + k) % NZ) for k in range(1, NZ)]
    partners += [net.at(x=(net.x + k) % NX) for k in range(1, NX)]
    partners += [net.at(core=other), net.at(z=z + 1 - 2 * net.half, core=other)]
    for dev in partners:
        pl.semaphore_signal(barrier, inc=1, device_id=dev, device_id_type=MESH)

    lane = iota((8, 128), 1)
    length = [lengths[i] for i in range(4)]
    group = [group_of[i] for i in range(4)]
    reward = [rewards[i].astype(F32) for i in range(4)]
    opening = [0 * length[0]]
    for i in range(3):
        opening.append(opening[-1] + length[i])
    info = jnp.where(lane == net.s, (opening[3] + length[3]).astype(F32), 0.0)
    for i in range(4):
        info += jnp.where(lane == 64 + group[i], reward[i], 0.0)
        info += jnp.where(lane == 96 + group[i], reward[i] * reward[i], 0.0)
    v["info_own"][...] = info
    pl.semaphore_wait(barrier, len(partners))

    @pl.when(net.core == 0)
    def _():
        product_core(
            Links(),
            (
                shard, gain, v["weights"], v["scaled"], v["raw"], v["product"], v["give"], v["take"], v["home"], v["squares"],
                hidden, v["hidden0"], v["terms"], states_out, terms_out,
            ),
            (m["swap"], m["pa"], m["pf"], m["pb"], m["a2"], m["b2"], m["r"], m["o"], own_sem),
        )

    @pl.when(net.core == 1)
    def _():
        names = (
            "info_own", "info_y", "info_line", "info_z", "send1", "r1a", "r1b", "s2a", "s2b", "r2a", "r2b",
            "full_rows", "terms", "squares_own", "squares", "take", "home", "raw",
        )
        token_core(
            Links(),
            (hidden, v["hidden0"], shard, old_logp, ref_logp, lengths, group_of, rewards, v["weights"])
            + tuple(v[n] for n in names)
            + (states_out, terms_out),
            (m["swap"], m["iy"], m["iz"], m["deliver"], m["x"], m["r"], m["o"], (info, length, group, reward, opening)),
        )


def shards(hidden, projection, norm_gain, old_logp, ref_logp, lengths, group_of, rewards):
    dma = pltpu.SemaphoreType.DMA
    vmem = pl.BlockSpec(memory_space=pltpu.VMEM)
    smem = pl.BlockSpec(memory_space=pltpu.SMEM)
    pairs = []
    for shape in SEMAPHORES.values():
        pairs += [dma(shape), dma(shape)]
    return pl.pallas_call(
        kernel,
        out_shape=(
            jax.ShapeDtypeStruct((TOK, COLS), BF16),
            jax.ShapeDtypeStruct((TOK, 2), BF16),
        ),
        in_specs=[vmem] * 5 + [smem] * 3,
        out_specs=(vmem, vmem),
        scratch_shapes=[pltpu.VMEM(*spec) for spec in SCRATCH.values()] + pairs + [dma((1,))],
        compiler_params=pltpu.CompilerParams(collective_id=0, has_side_effects=True),
    )(
        hidden,
        projection,
        norm_gain.reshape(1, D),
        old_logp.reshape(1, SLOTS),
        ref_logp.reshape(1, SLOTS),
        lengths,
        group_of,
        rewards,
    )


def solution(mesh):
    in_specs = (
        P("seq", ("sec", "tp")),
        P("seq", ("sec", "tp")),
        P(),
        P("seq"),
        P("seq"),
        P("seq"),
        P("seq"),
        P("seq"),
    )
    out_specs = (P("seq", ("sec", "tp")), P("seq", None))
    return jax.shard_map(shards, mesh=mesh, in_specs=in_specs, out_specs=out_specs, check_vma=False)
```

```python
import jax
import jax.numpy as jnp
from jax import lax
from jax.experimental import pallas as pl
from jax.experimental.pallas import tpu as pltpu
from jax.sharding import PartitionSpec as P

D = 5120
GROUP = 8
LMAX = 64
COLS = 640
BOTH = 2 * COLS
WROWS = 80
NX, NY, NZ = 4, 8, 8
NQ = NZ // 2
TOK = 128
SLOTS = 256
TERMS = 128
CUT = 384
WIDE = COLS + TERMS
WCUT = 768
F32 = jnp.float32
BF16 = jnp.bfloat16
MESH = pl.DeviceIdType.MESH
ORDER = (
    (2, 0, 1), (2, 1, 1), (3, 1, 0, 0), (3, 1, 1, 0), (0, 0), (0, 1), (2, 0, 2), (2, 1, 2),
    (4, 1, 0, 0), (3, 2, 0, 0), (3, 2, 1, 0), (3, 1, 0, 3), (3, 1, 1, 3), (4, 1, 1, 7), (3, 1, 0, 1), (3, 1, 1, 1),
    (4, 1, 0, 1), (2, 0, 3), (2, 1, 3), (1, 0), (1, 1), (3, 3, 0, 0), (3, 2, 0, 3), (3, 2, 1, 3),
    (4, 1, 1, 6), (3, 2, 0, 1), (3, 2, 1, 1), (2, 0, 4), (2, 1, 4), (4, 1, 0, 2), (3, 1, 0, 2), (3, 1, 1, 2),
    (3, 3, 1, 3), (4, 1, 1, 5), (3, 3, 0, 1), (3, 2, 1, 2), (3, 2, 0, 2), (4, 1, 0, 3), (3, 3, 1, 2), (4, 1, 1, 4),
)


def iota(shape, dim):
    return lax.broadcasted_iota(jnp.int32, shape, dim)


def one_hot(mask):
    return jnp.where(mask, 1.0, 0.0).astype(BF16)


def picked(table, rows):
    return jnp.dot(table, rows, preferred_element_type=F32).astype(BF16)


def flat(rows):
    return rows.reshape(SLOTS, rows.shape[-1])


def tiles(rows):
    return rows.reshape(8, 32, rows.shape[-1])


class Links:
    def __init__(self):
        self.x, self.s, self.core = (lax.axis_index(n) for n in ("sec", "seq", "tp"))
        self.y, self.z = self.s % NY, self.s // NY
        self.half, self.q = self.z % 2, self.z // 2
        self.pending = []

    def at(self, x=None, y=None, z=None, core=None):
        zz = self.z if z is None else z
        yy = self.y if y is None else y
        return {
            "sec": self.x if x is None else x,
            "seq": zz * NY + yy,
            "tp": self.core if core is None else core,
        }

    def remote(self, src, dst, sems, dev):
        return pltpu.make_async_remote_copy(
            src_ref=src, dst_ref=dst, send_sem=sems[0], recv_sem=sems[1], device_id=dev, device_id_type=MESH
        )

    def send(self, src, dst, sems, dev):
        copy = self.remote(src, dst, sems, dev)
        copy.start()
        self.pending.append(copy)

    def arrived(self, dst, sems):
        self.remote(dst, dst, sems, self.at(core=1 - self.core)).wait_recv()

    def finish(self):
        for copy in self.pending:
            copy.wait_send()


def pair(sems, *index):
    return sems[0].at[index], sems[1].at[index]


def product_core(net, refs, sems):
    shard, gain, weights, scaled, raw, product, give, take, home, squares, hidden, hidden0, terms, states_out, terms_out = refs
    swap_sem, pa, pf, pb, a2, b2, r_sem, o_sem, own_sem = sems
    x, y, z, q, half = net.x, net.y, net.z, net.q, net.half
    zm = z + 1 - 2 * half
    mate = net.at(core=1)

    def rows(qq, yy):
        return pl.ds(pl.multiple_of(qq * COLS + yy * WROWS, 16), WROWS)

    def wa(qq, yy):
        return weights.at[rows(qq, yy), pl.ds(0, WCUT)]

    def wb(qq, yy):
        return weights.at[rows(qq, yy), pl.ds(WCUT, BOTH - WCUT)]

    def wa_part(qq, yy, way):
        return weights.at[rows(qq, yy), pl.ds(way * WCUT // 2, WCUT // 2)]

    def wb_part(qq, yy, way):
        return weights.at[rows(qq, yy), pl.ds(WCUT + way * (BOTH - WCUT) // 2, (BOTH - WCUT) // 2)]

    y_way = net.at(y=(y + 1) % NY), net.at(y=(y + NY - 1) % NY)
    z_way = net.at(z=(z + 2) % NZ), net.at(z=(z + NZ - 2) % NZ)

    def along_y(j):
        piece = wa((q + j) % NQ, y)
        for way in (0, 1):
            net.send(piece, piece, pair(a2, way, 1, j), y_way[way])

    def along_z(j):
        piece = wb(q, (y + j) % NY)
        for way in (0, 1):
            net.send(piece, piece, pair(b2, way, 1, j), z_way[way])

    own = pltpu.make_async_copy(shard, weights.at[rows(q, y), pl.ds(0, COLS)], own_sem.at[0])
    own.start()
    net.send(hidden, hidden0, pair(swap_sem, 0), mate)
    own.wait()
    net.arrived(weights.at[rows(q, y), pl.ds(COLS, COLS)], pair(swap_sem, 1))
    for way in (0, 1):
        net.send(wa(q, y), wa(q, y), pair(pa, way), z_way[way])
    for way in (0, 1):
        net.send(wb(q, y), wb(q, y), pair(pb, way, 1), y_way[way])
    along_y(0)
    along_z(0)

    met = []

    def first_a(way):
        qq = (q + 3 - 2 * way) % NQ
        net.arrived(wa(qq, y), pair(pa, way))
        part = wa_part(qq, y, way)
        net.send(part, part, pair(pf, way), z_way[way])
        along_y(3 - 2 * way)

    def far_a(way):
        net.arrived(wa_part((q + 2) % NQ, y, way), pair(pf, way))
        if "far" in met:
            along_y(2)
        met.append("far")

    def first_b(way, d):
        yy = (y + (d if way else NY - d)) % NY
        part = wb_part(q, yy, way)
        piece = part if d == 4 else wb(q, yy)
        net.arrived(piece, pair(pb, way, d))
        if d < 3:
            net.send(piece, piece, pair(pb, way, d + 1), y_way[way])
        elif d == 3:
            net.send(part, part, pair(pb, way, 4), y_way[way])
        if d < 4:
            along_z(d if way else NY - d)
        elif "half" in met:
            along_z(4)
        else:
            met.append("half")

    waiting = [(3, d, way, j) for d in (1, 2, 3) for way in (0, 1) for j in range(NQ)]
    waiting += [(3, 4, j // 2, j) for j in range(NQ)]
    waiting += [(4, 1, way, j) for way in (0, 1) for j in range(NY)]
    waiting += [(4, 2, j // 4, j) for j in range(NY)]

    def next_a(d, way, j):
        waiting.remove((3, d, way, j))
        piece = wa((q + j) % NQ, (y + (d if way else NY - d)) % NY)
        net.arrived(piece, pair(a2, way, d, j))
        if d < 3 or (d == 3 and j // 2 == way):
            net.send(piece, piece, pair(a2, way, d + 1, j), y_way[way])

    def next_b(d, way, j):
        waiting.remove((4, d, way, j))
        piece = wb((q + (d if way else NQ - d)) % NQ, (y + j) % NY)
        net.arrived(piece, pair(b2, way, d, j))
        if d == 1 and j // 4 == way:
            net.send(piece, piece, pair(b2, way, 2, j), z_way[way])

    hops = (first_a, far_a, first_b, next_a, next_b)
    for kind, *index in ORDER:
        hops[kind](*index)

    for n, xx in enumerate((x, (x + NX - 1) % NX, (x + 1) % NX, (x + 2) % NX)):
        for i in range(2):
            net.arrived(raw.at[xx, pl.ds(i * TOK, TOK), :], pair(r_sem, n, i))
        g = gain[:, pl.ds(pl.multiple_of((2 * xx + half) * COLS, 128), COLS)]
        scaled[:, pl.ds(pl.multiple_of(xx * COLS, 128), COLS)] = (raw[xx].astype(F32) * g).astype(BF16)
    net.arrived(terms, pair(o_sem, 5))
    terms_out[...] = terms[:2, :]
    net.arrived(squares.at[0], pair(o_sem, 0))
    net.arrived(squares.at[1], pair(o_sem, 1))
    rate = lax.rsqrt((squares[0] + squares[1])[0:1] * (1.0 / D) + 1e-6)
    scale = jnp.sum(jnp.where(iota((SLOTS, 1), 0) == iota((1, SLOTS), 1), rate, 0.0), axis=1, keepdims=True)
    away = pl.ds(pl.multiple_of((1 - half) * TOK, TOK), TOK)
    near = pl.ds(pl.multiple_of(half * TOK, TOK), TOK)

    for c, kind in ((0, 3), (1, 4)):
        for item in [w for w in waiting if w[0] == kind]:
            hops[kind](*item[1:])
        cols = pl.ds(c * COLS, COLS)
        part = jnp.dot(scaled[...], weights[:, cols], preferred_element_type=F32)
        kept = jnp.where(half == c, 1.0, 0.0)
        product[:, cols] = part * scale + raw[x].astype(F32) * kept
        give[c] = product[away, cols].astype(BF16)
        net.send(give.at[c], take, pair(o_sem, 2 + c), net.at(z=zm, core=c))
    net.send(product.at[near, pl.ds(COLS, COLS)], home, pair(o_sem, 4), mate)
    net.arrived(take, pair(o_sem, 2))
    states_out[...] = (product[near, :COLS] + take[...].astype(F32)).astype(BF16)
    net.finish()


def token_core(net, refs, sems):
    (
        hidden, hidden0, shard, old_logp, ref_logp, lengths, group_of, rewards, weights,
        info_own, info_y, info_line, info_z, send1, r1a, r1b, s2a, s2b, r2a, r2b,
        full_rows, terms, squares_own, squares, take, home, raw, states_out, terms_out,
    ) = refs
    swap_sem, iy, iz, del_sem, x_sem, r_sem, o_sem, own_info = sems
    x, y, z, q, half, s = net.x, net.y, net.z, net.q, net.half, net.s
    zm = z + 1 - 2 * half
    mate = net.at(core=0)
    info, length, group, reward, opening = own_info

    for k in range(1, NY):
        net.send(info_own, info_y.at[k], pair(iy, k), net.at(y=(y + k) % NY))
    own_rows = pl.ds(pl.multiple_of(q * COLS + y * WROWS, 16), WROWS)
    net.send(shard, weights.at[own_rows, pl.ds(COLS, COLS)], pair(swap_sem, 1), mate)
    line = info
    for k in range(1, NY):
        net.arrived(info_y.at[k], pair(iy, k))
        line += info_y[k]
    info_line[...] = line
    for k in range(1, NZ):
        net.send(info_line, info_z.at[k], pair(iz, k), net.at(z=(z + k) % NZ))

    lane = iota((8, 128), 1)
    col = iota((1, SLOTS), 1)
    spot = jnp.full((1, SLOTS), -1, jnp.int32)
    for i in range(4):
        p = col - i * LMAX
        spot = jnp.where((p >= 0) & (p < length[i]), opening[i] + p, spot)
    row = iota((SLOTS, 1), 0)
    turned = ((row // 4 % 8) * 8 + row // 32) * 4 + row % 4
    ratio = ref_logp[...] - old_logp[...]
    penalty = jnp.exp(ratio) - ratio - 1.0
    pen_col = jnp.sum(jnp.where(row == col, penalty, 0.0), axis=1, keepdims=True)
    swap = one_hot(turned == col)
    net.arrived(hidden0, pair(swap_sem, 0))

    total = line
    for k in range(1, NZ):
        net.arrived(info_z.at[k], pair(iz, k))
        total += info_z[k]

    first = (jnp.sum(jnp.where(lane < s, total, 0.0)) * 0.125).astype(jnp.int32)
    table1 = one_hot((((turned - first) & (SLOTS - 1))) == spot)
    table2 = one_hot((((row - first) & (SLOTS - 1))) == spot)
    lanes1, lanes2 = pl.ds(0, CUT), pl.ds(CUT, WIDE - CUT)

    def route_y(n, src, dst, lanes):
        dst[:, y] = src[:, y, :, lanes]
        for k in (4, 3, 5, 2, 6, 1, 7):
            t = (y + k) % NY
            net.send(src.at[:, t, :, lanes], dst.at[:, y], pair(del_sem, n, k), net.at(y=t))

    def wait_y(n, dst):
        for k in range(1, NY):
            net.arrived(dst.at[:, (y + NY - k) % NY], pair(del_sem, n, k))

    def route_z(n, src, dst, lanes):
        dst[z] = src[half, pl.ds(2 * q, 2), :, lanes]
        for k in (4, 3, 5, 2, 6, 1, 7):
            t = (z + k) % NZ
            net.send(src.at[t % 2, pl.ds(2 * (t // 2), 2), :, lanes], dst.at[z], pair(del_sem, n, k), net.at(z=t))

    def wait_z(n, dst):
        for k in range(1, NZ):
            net.arrived(dst.at[(z + NZ - k) % NZ], pair(del_sem, n, k))

    send1[0, :, :, :CUT] = tiles(picked(table1, hidden0[:, :CUT]))
    send1[1, :, :, :CUT] = tiles(picked(table1, hidden[:, :CUT]))
    route_y(0, send1, r1a, lanes1)

    mean = total * (1.0 / GROUP)
    mean_square = pltpu.roll(mean, 96, 1)
    spread = jnp.maximum(jnp.sqrt(mean_square - mean * mean), 1.0)
    adv_col = jnp.zeros((SLOTS, 1), F32)
    for i in range(4):
        value = jnp.where(lane == 64 + group[i], (reward[i] - mean) / spread, 0.0)
        adv_col = jnp.where(row // LMAX == i, jnp.sum(value) * 0.125, adv_col)
    term_lane = iota((SLOTS, TERMS), 1)
    own_terms = jnp.where(term_lane == 0, adv_col, jnp.where(term_lane == 1, pen_col, 0.0)).astype(BF16)
    send1[0, :, :, CUT:COLS] = tiles(picked(table2, hidden0[:, CUT:]))
    send1[1, :, :, CUT:COLS] = tiles(picked(table2, hidden[:, CUT:]))
    moved = tiles(picked(table2, own_terms))
    send1[0, :, :, COLS:] = moved
    send1[1, :, :, COLS:] = moved
    route_z(1, send1, r1b, lanes2)

    counts = total.astype(BF16)
    sender = iota((128, SLOTS), 0)
    natural = iota((128, SLOTS), 1) // 4
    swapped = (natural % 8) * 8 + natural // 8
    w = iota((TOK, 1), 0)
    same = w % 4 == col % 4

    def bounds(order):
        low = jnp.dot(counts, one_hot(sender < order), preferred_element_type=F32)[0:1]
        high = jnp.dot(counts, one_hot(sender <= order), preferred_element_type=F32)[0:1]
        return low, high

    def pick_table(limits, e):
        packed = ((w // 4) * SLOTS + ((2 * q + e) * NY + y) * 4 + w % 4).astype(F32)
        return one_hot((limits[0] <= packed) & (packed < limits[1]) & same)

    limits1, limits2 = bounds(natural), bounds(swapped)
    pick1 = [pick_table(limits1, e) for e in range(2)]
    pick2 = [pick_table(limits2, e) for e in range(2)]

    whole = pl.ds(0, CUT)
    wait_y(0, r1a)
    for c in range(2):
        s2a[c] = tiles(picked(swap, flat(r1a[c])))
    route_z(2, s2a, r2a, whole)
    wait_z(1, r1b)
    for e in range(2):
        s2b[e] = tiles(picked(swap, flat(r1b[:, e])))
    route_y(3, s2b, r2b, whole)

    wait_z(2, r2a)
    for e in range(2):
        full_rows[x, e * TOK : (e + 1) * TOK, :CUT] = picked(pick1[e], flat(r2a[:, e]))
    wait_y(3, r2b)
    for e in range(2):
        full_rows[x, e * TOK : (e + 1) * TOK, CUT:] = picked(pick2[e], flat(r2b[e, :, :, : COLS - CUT]))

    x_up, x_dn = net.at(x=(x + 1) % NX), net.at(x=(x + NX - 1) % NX)
    x_l, x_r, x_f = (x + NX - 1) % NX, (x + 1) % NX, (x + 2) % NX

    def part(xx, i):
        return full_rows.at[xx, pl.ds(i * TOK, TOK), :]

    def over(xx, i, way, slot):
        net.send(part(xx, i), part(xx, i), pair(x_sem, way, slot), (x_up, x_dn)[way])

    def down(xx, n, i):
        net.send(part(xx, i), raw.at[xx, pl.ds(i * TOK, TOK), :], pair(r_sem, n, i), mate)

    over(x, 0, 0, 0)
    over(x, 1, 1, 1)
    over(x, 1, 0, 1)
    over(x, 0, 1, 0)
    down(x, 0, 0)
    down(x, 0, 1)
    chosen = jnp.where(half == 0, pick2[0].astype(F32), pick2[1].astype(F32)).astype(BF16)
    terms[...] = lax.dot_general(
        flat(r2b[half, :, :, COLS - CUT :]), chosen, (((0,), (1,)), ((), ())), preferred_element_type=F32
    ).astype(BF16)
    net.send(terms, terms, pair(o_sem, 5), mate)
    terms_out[...] = terms[:2, :]

    square = [jnp.zeros((2 * TOK, 128), F32)]

    def add_squares(xx):
        wide = full_rows[xx].astype(F32)
        for t in range(COLS // 128):
            tile = wide[:, t * 128 : (t + 1) * 128]
            square[0] += tile * tile

    add_squares(x)
    net.arrived(part(x_l, 0), pair(x_sem, 0, 0))
    over(x_l, 0, 0, 2)
    net.arrived(part(x_r, 1), pair(x_sem, 1, 1))
    over(x_r, 1, 1, 2)
    down(x_l, 1, 0)
    down(x_r, 2, 1)
    net.arrived(part(x_l, 1), pair(x_sem, 0, 1))
    down(x_l, 1, 1)
    net.arrived(part(x_r, 0), pair(x_sem, 1, 0))
    down(x_r, 2, 0)
    add_squares(x_l)
    add_squares(x_r)
    net.arrived(part(x_f, 0), pair(x_sem, 0, 2))
    down(x_f, 3, 0)
    net.arrived(part(x_f, 1), pair(x_sem, 1, 2))
    down(x_f, 3, 1)
    add_squares(x_f)
    squares_own[...] = lax.dot_general(
        jnp.ones((8, 128), F32), square[0], (((1,), (1,)), ((), ())),
        precision=lax.Precision.HIGHEST, preferred_element_type=F32,
    )
    net.send(squares_own, squares.at[0], pair(o_sem, 0), mate)
    net.send(squares_own, squares.at[1], pair(o_sem, 1), net.at(z=zm, core=0))

    net.arrived(home, pair(o_sem, 4))
    net.arrived(take, pair(o_sem, 3))
    states_out[...] = (home[...] + take[...].astype(F32)).astype(BF16)
    net.finish()


SCRATCH = dict(
    info_own=((8, 128), F32),
    info_y=((NY, 8, 128), F32),
    info_line=((8, 128), F32),
    info_z=((NZ, 8, 128), F32),
    send1=((2, 8, 32, WIDE), BF16),
    r1a=((2, 8, 32, CUT), BF16),
    r1b=((8, 2, 32, CUT), BF16),
    s2a=((2, 8, 32, CUT), BF16),
    s2b=((2, 8, 32, CUT), BF16),
    r2a=((8, 2, 32, CUT), BF16),
    r2b=((2, 8, 32, CUT), BF16),
    full_rows=((NX, 2 * TOK, COLS), BF16),
    raw=((NX, 2 * TOK, COLS), BF16),
    terms=((TERMS, TOK), BF16),
    hidden0=((SLOTS, COLS), BF16),
    weights=((NQ * COLS, BOTH), BF16),
    scaled=((2 * TOK, NX * COLS), BF16),
    product=((2 * TOK, BOTH), F32),
    give=((2, TOK, COLS), BF16),
    take=((TOK, COLS), BF16),
    home=((TOK, COLS), F32),
    squares_own=((8, 2 * TOK), F32),
    squares=((2, 8, 2 * TOK), F32),
    hidden=((SLOTS, COLS), BF16),
    shard=((WROWS, COLS), BF16),
    gain=((1, D), F32),
    old_logp=((1, SLOTS), F32),
    ref_logp=((1, SLOTS), F32),
)
INPUTS = ["hidden", "shard", "gain", "old_logp", "ref_logp"]
SEMAPHORES = dict(
    swap=(2,),
    iy=(8,),
    iz=(8,),
    deliver=(4, 8),
    pa=(2,),
    pf=(2,),
    pb=(2, 5),
    a2=(2, 5, 4),
    b2=(2, 3, 8),
    x=(2, 3),
    r=(4, 2),
    o=(6,),
)


def kernel(*refs):
    inputs, (states_out, terms_out), rest = refs[:8], refs[8:10], refs[10:]
    v = dict(zip(SCRATCH, rest))
    sem_refs = rest[len(SCRATCH) :]
    m = {n: (sem_refs[2 * i], sem_refs[2 * i + 1]) for i, n in enumerate(SEMAPHORES)}
    own_sem, in_sem, *scalars = sem_refs[2 * len(SEMAPHORES) :]
    hidden, shard, gain, old_logp, ref_logp = (v[n] for n in INPUTS)
    lengths, group_of, rewards = scalars

    net = Links()
    y, z = net.y, net.z
    other = 1 - net.core
    barrier = pltpu.get_barrier_semaphore()
    partners = [net.at(y=(y + k) % NY) for k in range(1, NY)]
    partners += [net.at(z=(z + k) % NZ) for k in range(1, NZ)]
    partners += [net.at(x=(net.x + k) % NX) for k in range(1, NX)]
    partners += [net.at(core=other), net.at(z=z + 1 - 2 * net.half, core=other)]
    for dev in partners:
        pl.semaphore_signal(barrier, inc=1, device_id=dev, device_id_type=MESH)

    loads = []
    for i, dst in enumerate([hidden, shard, gain, old_logp, ref_logp, lengths, group_of, rewards]):
        loads.append(pltpu.make_async_copy(inputs[i], dst, in_sem.at[i]))
    for i in (5, 6, 7, 0, 1, 2, 3, 4):
        loads[i].start()
    for i in (5, 6, 7, 0, 1, 2, 3, 4):
        loads[i].wait()
    lane = iota((8, 128), 1)
    length = [lengths[i] for i in range(4)]
    group = [group_of[i] for i in range(4)]
    reward = [rewards[i].astype(F32) for i in range(4)]
    opening = [0 * length[0]]
    for i in range(3):
        opening.append(opening[-1] + length[i])
    info = jnp.where(lane == net.s, (opening[3] + length[3]).astype(F32), 0.0)
    for i in range(4):
        info += jnp.where(lane == 64 + group[i], reward[i], 0.0)
        info += jnp.where(lane == 96 + group[i], reward[i] * reward[i], 0.0)
    v["info_own"][...] = info
    pl.semaphore_wait(barrier, len(partners))

    @pl.when(net.core == 0)
    def _():
        product_core(
            Links(),
            (
                shard, gain, v["weights"], v["scaled"], v["raw"], v["product"], v["give"], v["take"], v["home"], v["squares"],
                hidden, v["hidden0"], v["terms"], states_out, terms_out,
            ),
            (m["swap"], m["pa"], m["pf"], m["pb"], m["a2"], m["b2"], m["r"], m["o"], own_sem),
        )

    @pl.when(net.core == 1)
    def _():
        names = (
            "info_own", "info_y", "info_line", "info_z", "send1", "r1a", "r1b", "s2a", "s2b", "r2a", "r2b",
            "full_rows", "terms", "squares_own", "squares", "take", "home", "raw",
        )
        token_core(
            Links(),
            (hidden, v["hidden0"], shard, old_logp, ref_logp, lengths, group_of, rewards, v["weights"])
            + tuple(v[n] for n in names)
            + (states_out, terms_out),
            (m["swap"], m["iy"], m["iz"], m["deliver"], m["x"], m["r"], m["o"], (info, length, group, reward, opening)),
        )


def handed_on(states, terms, states_out, terms_out):
    states_out[...] = states[...]
    terms_out[...] = terms[...]


def shards(hidden, projection, norm_gain, old_logp, ref_logp, lengths, group_of, rewards):
    dma = pltpu.SemaphoreType.DMA
    vmem = pl.BlockSpec(memory_space=pltpu.VMEM)
    anywhere = pl.BlockSpec(memory_space=pltpu.MemorySpace.HBM)
    pairs = []
    for shape in SEMAPHORES.values():
        pairs += [dma(shape), dma(shape)]
    states, terms = pl.pallas_call(
        kernel,
        out_shape=(
            jax.ShapeDtypeStruct((TOK, COLS), BF16),
            jax.ShapeDtypeStruct((2, TOK), BF16),
        ),
        in_specs=[anywhere] * 8,
        out_specs=(vmem, vmem),
        scratch_shapes=[pltpu.VMEM(*spec) for spec in SCRATCH.values()] + pairs
        + [dma((1,)), dma((8,))]
        + [pltpu.SMEM((4,), jnp.int32)] * 3,
        compiler_params=pltpu.CompilerParams(collective_id=0, has_side_effects=True),
    )(
        hidden,
        projection,
        norm_gain.reshape(1, D),
        old_logp.reshape(1, SLOTS),
        ref_logp.reshape(1, SLOTS),
        lengths,
        group_of,
        rewards,
    )
    states, terms = pl.pallas_call(
        handed_on,
        out_shape=(jax.ShapeDtypeStruct((TOK, COLS), BF16), jax.ShapeDtypeStruct((2, TOK), BF16)),
        in_specs=[vmem] * 2,
        out_specs=(vmem, vmem),
    )(states, terms)
    return states, terms.T


def solution(mesh):
    in_specs = (
        P("seq", ("sec", "tp")),
        P("seq", ("sec", "tp")),
        P(),
        P("seq"),
        P("seq"),
        P("seq"),
        P("seq"),
        P("seq"),
    )
    out_specs = (P("seq", ("sec", "tp")), P("seq", None))
    return jax.shard_map(shards, mesh=mesh, in_specs=in_specs, out_specs=out_specs, check_vma=False)
```

```python
import jax
import jax.numpy as jnp
from jax import lax
from jax.experimental import pallas as pl
from jax.experimental.pallas import tpu as pltpu
from jax.sharding import PartitionSpec as P

D = 5120
GROUP = 8
LMAX = 64
COLS = 640
BOTH = 2 * COLS
WROWS = 80
NX, NY, NZ = 4, 8, 8
NQ = NZ // 2
TOK = 128
SLOTS = 256
TERMS = 128
CUT = 384
WIDE = COLS + TERMS
WCUT = 768
F32 = jnp.float32
BF16 = jnp.bfloat16
MESH = pl.DeviceIdType.MESH
ORDER = (
    (2, 0, 1), (2, 1, 1), (3, 1, 0, 0), (3, 1, 1, 0), (0, 0), (0, 1), (2, 0, 2), (2, 1, 2),
    (4, 1, 0, 0), (3, 2, 0, 0), (3, 2, 1, 0), (4, 1, 1, 7), (3, 1, 0, 3), (3, 1, 1, 3), (3, 1, 0, 1), (3, 1, 1, 1),
    (4, 1, 0, 1), (2, 0, 3), (2, 1, 3), (1, 0), (1, 1), (3, 3, 0, 0), (4, 1, 1, 6), (3, 2, 0, 3),
    (3, 2, 1, 3), (3, 2, 0, 1), (3, 2, 1, 1), (4, 1, 0, 2), (2, 0, 4), (2, 1, 4), (3, 1, 0, 2), (3, 1, 1, 2),
    (3, 3, 1, 3), (4, 1, 1, 5), (3, 3, 0, 1), (3, 2, 1, 2), (3, 2, 0, 2), (4, 1, 0, 3), (4, 1, 1, 4), (3, 3, 1, 2),
)


def iota(shape, dim):
    return lax.broadcasted_iota(jnp.int32, shape, dim)


def one_hot(mask):
    return jnp.where(mask, 1.0, 0.0).astype(BF16)


def picked(table, rows):
    return jnp.dot(table, rows, preferred_element_type=F32).astype(BF16)


def flat(rows):
    return rows.reshape(SLOTS, rows.shape[-1])


def tiles(rows):
    return rows.reshape(8, 32, rows.shape[-1])


class Links:
    def __init__(self):
        self.x, self.s, self.core = (lax.axis_index(n) for n in ("sec", "seq", "tp"))
        self.y, self.z = self.s % NY, self.s // NY
        self.half, self.q = self.z % 2, self.z // 2
        self.pending = []

    def at(self, x=None, y=None, z=None, core=None):
        zz = self.z if z is None else z
        yy = self.y if y is None else y
        return {
            "sec": self.x if x is None else x,
            "seq": zz * NY + yy,
            "tp": self.core if core is None else core,
        }

    def remote(self, src, dst, sems, dev):
        return pltpu.make_async_remote_copy(
            src_ref=src, dst_ref=dst, send_sem=sems[0], recv_sem=sems[1], device_id=dev, device_id_type=MESH
        )

    def send(self, src, dst, sems, dev):
        copy = self.remote(src, dst, sems, dev)
        copy.start()
        self.pending.append(copy)

    def arrived(self, dst, sems):
        self.remote(dst, dst, sems, self.at(core=1 - self.core)).wait_recv()

    def finish(self):
        for copy in self.pending:
            copy.wait_send()


def pair(sems, *index):
    return sems[0].at[index], sems[1].at[index]


def product_core(net, refs, sems):
    shard, gain, weights, scaled, raw, product, give, take, home, squares, hidden, hidden0, terms, states_out, terms_out = refs
    swap_sem, pa, pf, pb, a2, b2, r_sem, o_sem, own_sem = sems
    x, y, z, q, half = net.x, net.y, net.z, net.q, net.half
    zm = z + 1 - 2 * half
    mate = net.at(core=1)

    def rows(qq, yy):
        return pl.ds(pl.multiple_of(qq * COLS + yy * WROWS, 16), WROWS)

    def wa(qq, yy):
        return weights.at[rows(qq, yy), pl.ds(0, WCUT)]

    def wb(qq, yy):
        return weights.at[rows(qq, yy), pl.ds(WCUT, BOTH - WCUT)]

    def wa_part(qq, yy, way):
        return weights.at[rows(qq, yy), pl.ds(way * WCUT // 2, WCUT // 2)]

    def wb_part(qq, yy, way):
        return weights.at[rows(qq, yy), pl.ds(WCUT + way * (BOTH - WCUT) // 2, (BOTH - WCUT) // 2)]

    y_way = net.at(y=(y + 1) % NY), net.at(y=(y + NY - 1) % NY)
    z_way = net.at(z=(z + 2) % NZ), net.at(z=(z + NZ - 2) % NZ)

    def along_y(j):
        piece = wa((q + j) % NQ, y)
        for way in (0, 1):
            net.send(piece, piece, pair(a2, way, 1, j), y_way[way])

    def along_z(j):
        piece = wb(q, (y + j) % NY)
        for way in (0, 1):
            net.send(piece, piece, pair(b2, way, 1, j), z_way[way])

    own = pltpu.make_async_copy(shard, weights.at[rows(q, y), pl.ds(0, COLS)], own_sem.at[0])
    own.start()
    net.send(hidden, hidden0, pair(swap_sem, 0), mate)
    own.wait()
    net.arrived(weights.at[rows(q, y), pl.ds(COLS, COLS)], pair(swap_sem, 1))
    for way in (0, 1):
        net.send(wa(q, y), wa(q, y), pair(pa, way), z_way[way])
    for way in (0, 1):
        net.send(wb(q, y), wb(q, y), pair(pb, way, 1), y_way[way])
    along_y(0)
    along_z(0)

    met = []

    def first_a(way):
        qq = (q + 3 - 2 * way) % NQ
        net.arrived(wa(qq, y), pair(pa, way))
        part = wa_part(qq, y, way)
        net.send(part, part, pair(pf, way), z_way[way])
        along_y(3 - 2 * way)

    def far_a(way):
        net.arrived(wa_part((q + 2) % NQ, y, way), pair(pf, way))
        if "far" in met:
            along_y(2)
        met.append("far")

    def first_b(way, d):
        yy = (y + (d if way else NY - d)) % NY
        part = wb_part(q, yy, way)
        piece = part if d == 4 else wb(q, yy)
        net.arrived(piece, pair(pb, way, d))
        if d < 3:
            net.send(piece, piece, pair(pb, way, d + 1), y_way[way])
        elif d == 3:
            net.send(part, part, pair(pb, way, 4), y_way[way])
        if d < 4:
            along_z(d if way else NY - d)
        elif "half" in met:
            along_z(4)
        else:
            met.append("half")

    waiting = [(3, d, way, j) for d in (1, 2, 3) for way in (0, 1) for j in range(NQ)]
    waiting += [(3, 4, j // 2, j) for j in range(NQ)]
    waiting += [(4, 1, way, j) for way in (0, 1) for j in range(NY)]
    waiting += [(4, 2, j // 4, j) for j in range(NY)]

    def next_a(d, way, j):
        waiting.remove((3, d, way, j))
        piece = wa((q + j) % NQ, (y + (d if way else NY - d)) % NY)
        net.arrived(piece, pair(a2, way, d, j))
        if d < 3 or (d == 3 and j // 2 == way):
            net.send(piece, piece, pair(a2, way, d + 1, j), y_way[way])

    def next_b(d, way, j):
        waiting.remove((4, d, way, j))
        piece = wb((q + (d if way else NQ - d)) % NQ, (y + j) % NY)
        net.arrived(piece, pair(b2, way, d, j))
        if d == 1 and j // 4 == way:
            net.send(piece, piece, pair(b2, way, 2, j), z_way[way])

    hops = (first_a, far_a, first_b, next_a, next_b)
    for kind, *index in ORDER:
        hops[kind](*index)

    for n, xx in enumerate((x, (x + NX - 1) % NX, (x + 1) % NX, (x + 2) % NX)):
        for i in range(2):
            net.arrived(raw.at[xx, pl.ds(i * TOK, TOK), :], pair(r_sem, n, i))
        g = gain[:, pl.ds(pl.multiple_of((2 * xx + half) * COLS, 128), COLS)]
        scaled[:, pl.ds(pl.multiple_of(xx * COLS, 128), COLS)] = (raw[xx].astype(F32) * g).astype(BF16)
    net.arrived(terms, pair(o_sem, 5))
    terms_out[...] = terms[:2, :]
    net.arrived(squares.at[0], pair(o_sem, 0))
    net.arrived(squares.at[1], pair(o_sem, 1))
    rate = lax.rsqrt((squares[0] + squares[1])[0:1] * (1.0 / D) + 1e-6)
    scale = jnp.sum(jnp.where(iota((SLOTS, 1), 0) == iota((1, SLOTS), 1), rate, 0.0), axis=1, keepdims=True)
    away = pl.ds(pl.multiple_of((1 - half) * TOK, TOK), TOK)
    near = pl.ds(pl.multiple_of(half * TOK, TOK), TOK)

    def arrive(kind):
        for item in [w for w in waiting if w[0] == kind]:
            hops[kind](*item[1:])

    def refine(c, start, width, slot):
        cols, own_cols = pl.ds(c * COLS + start, width), pl.ds(start, width)
        part = jnp.dot(scaled[...], weights[:, cols], preferred_element_type=F32)
        kept = jnp.where(half == c, 1.0, 0.0)
        product[:, cols] = part * scale + raw[x, :, own_cols].astype(F32) * kept
        give[c, :, own_cols] = product[away, cols].astype(BF16)
        net.send(give.at[c, :, own_cols], take.at[:, own_cols], pair(o_sem, slot), net.at(z=zm, core=c))

    arrive(4)
    refine(1, WCUT - COLS, BOTH - WCUT, 3)
    arrive(3)
    refine(1, 0, WCUT - COLS, 6)
    refine(0, 0, COLS, 2)
    net.send(product.at[near, pl.ds(COLS, COLS)], home, pair(o_sem, 4), mate)
    net.arrived(take, pair(o_sem, 2))
    states_out[...] = (product[near, :COLS] + take[...].astype(F32)).astype(BF16)
    net.finish()


def token_core(net, refs, sems):
    (
        hidden, hidden0, shard, old_logp, ref_logp, lengths, group_of, rewards, weights,
        info_own, info_y, info_line, info_z, send1, r1a, r1b, s2a, s2b, r2a, r2b,
        full_rows, terms, squares_own, squares, take, home, raw, states_out, terms_out,
    ) = refs
    swap_sem, iy, iz, del_sem, x_sem, r_sem, o_sem, own_info = sems
    x, y, z, q, half, s = net.x, net.y, net.z, net.q, net.half, net.s
    zm = z + 1 - 2 * half
    mate = net.at(core=0)
    info, length, group, reward, opening = own_info

    for k in range(1, NY):
        net.send(info_own, info_y.at[k], pair(iy, k), net.at(y=(y + k) % NY))
    own_rows = pl.ds(pl.multiple_of(q * COLS + y * WROWS, 16), WROWS)
    net.send(shard, weights.at[own_rows, pl.ds(COLS, COLS)], pair(swap_sem, 1), mate)
    line = info
    for k in range(1, NY):
        net.arrived(info_y.at[k], pair(iy, k))
        line += info_y[k]
    info_line[...] = line
    for k in range(1, NZ):
        net.send(info_line, info_z.at[k], pair(iz, k), net.at(z=(z + k) % NZ))

    lane = iota((8, 128), 1)
    col = iota((1, SLOTS), 1)
    spot = jnp.full((1, SLOTS), -1, jnp.int32)
    for i in range(4):
        p = col - i * LMAX
        spot = jnp.where((p >= 0) & (p < length[i]), opening[i] + p, spot)
    row = iota((SLOTS, 1), 0)
    turned = ((row // 4 % 8) * 8 + row // 32) * 4 + row % 4
    ratio = ref_logp[...] - old_logp[...]
    penalty = jnp.exp(ratio) - ratio - 1.0
    pen_col = jnp.sum(jnp.where(row == col, penalty, 0.0), axis=1, keepdims=True)
    swap = one_hot(turned == col)
    net.arrived(hidden0, pair(swap_sem, 0))

    total = line
    for k in range(1, NZ):
        net.arrived(info_z.at[k], pair(iz, k))
        total += info_z[k]

    first = (jnp.sum(jnp.where(lane < s, total, 0.0)) * 0.125).astype(jnp.int32)
    table1 = one_hot((((turned - first) & (SLOTS - 1))) == spot)
    table2 = one_hot((((row - first) & (SLOTS - 1))) == spot)
    lanes1, lanes2 = pl.ds(0, CUT), pl.ds(CUT, WIDE - CUT)

    def route_y(n, src, dst, lanes):
        dst[:, y] = src[:, y, :, lanes]
        for k in (4, 3, 5, 2, 6, 1, 7):
            t = (y + k) % NY
            net.send(src.at[:, t, :, lanes], dst.at[:, y], pair(del_sem, n, k), net.at(y=t))

    def wait_y(n, dst):
        for k in range(1, NY):
            net.arrived(dst.at[:, (y + NY - k) % NY], pair(del_sem, n, k))

    def route_z(n, src, dst, lanes):
        dst[z] = src[half, pl.ds(2 * q, 2), :, lanes]
        for k in (4, 3, 5, 2, 6, 1, 7):
            t = (z + k) % NZ
            net.send(src.at[t % 2, pl.ds(2 * (t // 2), 2), :, lanes], dst.at[z], pair(del_sem, n, k), net.at(z=t))

    def wait_z(n, dst):
        for k in range(1, NZ):
            net.arrived(dst.at[(z + NZ - k) % NZ], pair(del_sem, n, k))

    send1[0, :, :, :CUT] = tiles(picked(table1, hidden0[:, :CUT]))
    send1[1, :, :, :CUT] = tiles(picked(table1, hidden[:, :CUT]))
    route_y(0, send1, r1a, lanes1)

    mean = total * (1.0 / GROUP)
    mean_square = pltpu.roll(mean, 96, 1)
    spread = jnp.maximum(jnp.sqrt(mean_square - mean * mean), 1.0)
    adv_col = jnp.zeros((SLOTS, 1), F32)
    for i in range(4):
        value = jnp.where(lane == 64 + group[i], (reward[i] - mean) / spread, 0.0)
        adv_col = jnp.where(row // LMAX == i, jnp.sum(value) * 0.125, adv_col)
    term_lane = iota((SLOTS, TERMS), 1)
    own_terms = jnp.where(term_lane == 0, adv_col, jnp.where(term_lane == 1, pen_col, 0.0)).astype(BF16)
    send1[0, :, :, CUT:COLS] = tiles(picked(table2, hidden0[:, CUT:]))
    send1[1, :, :, CUT:COLS] = tiles(picked(table2, hidden[:, CUT:]))
    moved = tiles(picked(table2, own_terms))
    send1[0, :, :, COLS:] = moved
    send1[1, :, :, COLS:] = moved
    route_z(1, send1, r1b, lanes2)

    counts = total.astype(BF16)
    sender = iota((128, SLOTS), 0)
    natural = iota((128, SLOTS), 1) // 4
    swapped = (natural % 8) * 8 + natural // 8
    w = iota((TOK, 1), 0)
    same = w % 4 == col % 4

    def bounds(order):
        low = jnp.dot(counts, one_hot(sender < order), preferred_element_type=F32)[0:1]
        high = jnp.dot(counts, one_hot(sender <= order), preferred_element_type=F32)[0:1]
        return low, high

    def pick_table(limits, e):
        packed = ((w // 4) * SLOTS + ((2 * q + e) * NY + y) * 4 + w % 4).astype(F32)
        return one_hot((limits[0] <= packed) & (packed < limits[1]) & same)

    limits1, limits2 = bounds(natural), bounds(swapped)
    pick1 = [pick_table(limits1, e) for e in range(2)]
    pick2 = [pick_table(limits2, e) for e in range(2)]

    whole = pl.ds(0, CUT)
    wait_y(0, r1a)
    for c in range(2):
        s2a[c] = tiles(picked(swap, flat(r1a[c])))
    route_z(2, s2a, r2a, whole)
    wait_z(1, r1b)
    for e in range(2):
        s2b[e] = tiles(picked(swap, flat(r1b[:, e])))
    route_y(3, s2b, r2b, whole)

    wait_z(2, r2a)
    for e in range(2):
        full_rows[x, e * TOK : (e + 1) * TOK, :CUT] = picked(pick1[e], flat(r2a[:, e]))
    wait_y(3, r2b)
    for e in range(2):
        full_rows[x, e * TOK : (e + 1) * TOK, CUT:] = picked(pick2[e], flat(r2b[e, :, :, : COLS - CUT]))

    x_up, x_dn = net.at(x=(x + 1) % NX), net.at(x=(x + NX - 1) % NX)
    x_l, x_r, x_f = (x + NX - 1) % NX, (x + 1) % NX, (x + 2) % NX

    def part(xx, i):
        return full_rows.at[xx, pl.ds(i * TOK, TOK), :]

    def over(xx, i, way, slot):
        net.send(part(xx, i), part(xx, i), pair(x_sem, way, slot), (x_up, x_dn)[way])

    def down(xx, n, i):
        net.send(part(xx, i), raw.at[xx, pl.ds(i * TOK, TOK), :], pair(r_sem, n, i), mate)

    over(x, 0, 0, 0)
    over(x, 1, 1, 1)
    over(x, 1, 0, 1)
    over(x, 0, 1, 0)
    down(x, 0, 0)
    down(x, 0, 1)
    chosen = jnp.where(half == 0, pick2[0].astype(F32), pick2[1].astype(F32)).astype(BF16)
    terms[...] = lax.dot_general(
        flat(r2b[half, :, :, COLS - CUT :]), chosen, (((0,), (1,)), ((), ())), preferred_element_type=F32
    ).astype(BF16)
    net.send(terms, terms, pair(o_sem, 5), mate)
    terms_out[...] = terms[:2, :]

    square = [jnp.zeros((2 * TOK, 128), F32)]

    def add_squares(xx):
        wide = full_rows[xx].astype(F32)
        for t in range(COLS // 128):
            tile = wide[:, t * 128 : (t + 1) * 128]
            square[0] += tile * tile

    add_squares(x)
    net.arrived(part(x_l, 0), pair(x_sem, 0, 0))
    over(x_l, 0, 0, 2)
    net.arrived(part(x_r, 1), pair(x_sem, 1, 1))
    over(x_r, 1, 1, 2)
    down(x_l, 1, 0)
    down(x_r, 2, 1)
    net.arrived(part(x_l, 1), pair(x_sem, 0, 1))
    down(x_l, 1, 1)
    net.arrived(part(x_r, 0), pair(x_sem, 1, 0))
    down(x_r, 2, 0)
    add_squares(x_l)
    add_squares(x_r)
    net.arrived(part(x_f, 0), pair(x_sem, 0, 2))
    down(x_f, 3, 0)
    net.arrived(part(x_f, 1), pair(x_sem, 1, 2))
    down(x_f, 3, 1)
    add_squares(x_f)
    squares_own[...] = lax.dot_general(
        jnp.ones((8, 128), F32), square[0], (((1,), (1,)), ((), ())),
        precision=lax.Precision.HIGHEST, preferred_element_type=F32,
    )
    net.send(squares_own, squares.at[0], pair(o_sem, 0), mate)
    net.send(squares_own, squares.at[1], pair(o_sem, 1), net.at(z=zm, core=0))

    net.arrived(home, pair(o_sem, 4))
    net.arrived(take.at[:, pl.ds(WCUT - COLS, BOTH - WCUT)], pair(o_sem, 3))
    net.arrived(take.at[:, pl.ds(0, WCUT - COLS)], pair(o_sem, 6))
    states_out[...] = (home[...] + take[...].astype(F32)).astype(BF16)
    net.finish()


SCRATCH = dict(
    info_own=((8, 128), F32),
    info_y=((NY, 8, 128), F32),
    info_line=((8, 128), F32),
    info_z=((NZ, 8, 128), F32),
    send1=((2, 8, 32, WIDE), BF16),
    r1a=((2, 8, 32, CUT), BF16),
    r1b=((8, 2, 32, CUT), BF16),
    s2a=((2, 8, 32, CUT), BF16),
    s2b=((2, 8, 32, CUT), BF16),
    r2a=((8, 2, 32, CUT), BF16),
    r2b=((2, 8, 32, CUT), BF16),
    full_rows=((NX, 2 * TOK, COLS), BF16),
    raw=((NX, 2 * TOK, COLS), BF16),
    terms=((TERMS, TOK), BF16),
    hidden0=((SLOTS, COLS), BF16),
    weights=((NQ * COLS, BOTH), BF16),
    scaled=((2 * TOK, NX * COLS), BF16),
    product=((2 * TOK, BOTH), F32),
    give=((2, TOK, COLS), BF16),
    take=((TOK, COLS), BF16),
    home=((TOK, COLS), F32),
    squares_own=((8, 2 * TOK), F32),
    squares=((2, 8, 2 * TOK), F32),
    hidden=((SLOTS, COLS), BF16),
    shard=((WROWS, COLS), BF16),
    gain=((1, D), F32),
    old_logp=((1, SLOTS), F32),
    ref_logp=((1, SLOTS), F32),
)
INPUTS = ["hidden", "shard", "gain", "old_logp", "ref_logp"]
SEMAPHORES = dict(
    swap=(2,),
    iy=(8,),
    iz=(8,),
    deliver=(4, 8),
    pa=(2,),
    pf=(2,),
    pb=(2, 5),
    a2=(2, 5, 4),
    b2=(2, 3, 8),
    x=(2, 3),
    r=(4, 2),
    o=(7,),
)


def kernel(*refs):
    inputs, (states_out, terms_out), rest = refs[:8], refs[8:10], refs[10:]
    v = dict(zip(SCRATCH, rest))
    sem_refs = rest[len(SCRATCH) :]
    m = {n: (sem_refs[2 * i], sem_refs[2 * i + 1]) for i, n in enumerate(SEMAPHORES)}
    own_sem, in_sem, *scalars = sem_refs[2 * len(SEMAPHORES) :]
    hidden, shard, gain, old_logp, ref_logp = (v[n] for n in INPUTS)
    lengths, group_of, rewards = scalars

    net = Links()
    y, z = net.y, net.z
    other = 1 - net.core
    barrier = pltpu.get_barrier_semaphore()
    partners = [net.at(y=(y + k) % NY) for k in range(1, NY)]
    partners += [net.at(z=(z + k) % NZ) for k in range(1, NZ)]
    partners += [net.at(x=(net.x + k) % NX) for k in range(1, NX)]
    partners += [net.at(core=other), net.at(z=z + 1 - 2 * net.half, core=other)]
    for dev in partners:
        pl.semaphore_signal(barrier, inc=1, device_id=dev, device_id_type=MESH)

    loads = []
    for i, dst in enumerate([hidden, shard, gain, old_logp, ref_logp, lengths, group_of, rewards]):
        loads.append(pltpu.make_async_copy(inputs[i], dst, in_sem.at[i]))
    for i in (5, 6, 7, 0, 1, 2, 3, 4):
        loads[i].start()
    for i in (5, 6, 7, 0, 1, 2, 3, 4):
        loads[i].wait()
    lane = iota((8, 128), 1)
    length = [lengths[i] for i in range(4)]
    group = [group_of[i] for i in range(4)]
    reward = [rewards[i].astype(F32) for i in range(4)]
    opening = [0 * length[0]]
    for i in range(3):
        opening.append(opening[-1] + length[i])
    info = jnp.where(lane == net.s, (opening[3] + length[3]).astype(F32), 0.0)
    for i in range(4):
        info += jnp.where(lane == 64 + group[i], reward[i], 0.0)
        info += jnp.where(lane == 96 + group[i], reward[i] * reward[i], 0.0)
    v["info_own"][...] = info
    pl.semaphore_wait(barrier, len(partners))

    @pl.when(net.core == 0)
    def _():
        product_core(
            Links(),
            (
                shard, gain, v["weights"], v["scaled"], v["raw"], v["product"], v["give"], v["take"], v["home"], v["squares"],
                hidden, v["hidden0"], v["terms"], states_out, terms_out,
            ),
            (m["swap"], m["pa"], m["pf"], m["pb"], m["a2"], m["b2"], m["r"], m["o"], own_sem),
        )

    @pl.when(net.core == 1)
    def _():
        names = (
            "info_own", "info_y", "info_line", "info_z", "send1", "r1a", "r1b", "s2a", "s2b", "r2a", "r2b",
            "full_rows", "terms", "squares_own", "squares", "take", "home", "raw",
        )
        token_core(
            Links(),
            (hidden, v["hidden0"], shard, old_logp, ref_logp, lengths, group_of, rewards, v["weights"])
            + tuple(v[n] for n in names)
            + (states_out, terms_out),
            (m["swap"], m["iy"], m["iz"], m["deliver"], m["x"], m["r"], m["o"], (info, length, group, reward, opening)),
        )


def handed_on(states, terms, states_out, terms_out):
    states_out[...] = states[...]
    terms_out[...] = terms[...]


def shards(hidden, projection, norm_gain, old_logp, ref_logp, lengths, group_of, rewards):
    dma = pltpu.SemaphoreType.DMA
    vmem = pl.BlockSpec(memory_space=pltpu.VMEM)
    anywhere = pl.BlockSpec(memory_space=pltpu.MemorySpace.HBM)
    pairs = []
    for shape in SEMAPHORES.values():
        pairs += [dma(shape), dma(shape)]
    states, terms = pl.pallas_call(
        kernel,
        out_shape=(
            jax.ShapeDtypeStruct((TOK, COLS), BF16),
            jax.ShapeDtypeStruct((2, TOK), BF16),
        ),
        in_specs=[anywhere] * 8,
        out_specs=(vmem, vmem),
        scratch_shapes=[pltpu.VMEM(*spec) for spec in SCRATCH.values()] + pairs
        + [dma((1,)), dma((8,))]
        + [pltpu.SMEM((4,), jnp.int32)] * 3,
        compiler_params=pltpu.CompilerParams(collective_id=0, has_side_effects=True),
    )(
        hidden,
        projection,
        norm_gain.reshape(1, D),
        old_logp.reshape(1, SLOTS),
        ref_logp.reshape(1, SLOTS),
        lengths,
        group_of,
        rewards,
    )
    states, terms = pl.pallas_call(
        handed_on,
        out_shape=(jax.ShapeDtypeStruct((TOK, COLS), BF16), jax.ShapeDtypeStruct((2, TOK), BF16)),
        in_specs=[vmem] * 2,
        out_specs=(vmem, vmem),
    )(states, terms)
    return states, terms.T


def solution(mesh):
    in_specs = (
        P("seq", ("sec", "tp")),
        P("seq", ("sec", "tp")),
        P(),
        P("seq"),
        P("seq"),
        P("seq"),
        P("seq"),
        P("seq"),
    )
    out_specs = (P("seq", ("sec", "tp")), P("seq", None))
    return jax.shard_map(shards, mesh=mesh, in_specs=in_specs, out_specs=out_specs, check_vma=False)
```

```python
import jax
import jax.numpy as jnp
from jax import lax
from jax.experimental import pallas as pl
from jax.experimental.pallas import tpu as pltpu
from jax.sharding import PartitionSpec as P

D = 5120
GROUP = 8
LMAX = 64
COLS = 640
BOTH = 2 * COLS
WROWS = 80
NX, NY, NZ = 4, 8, 8
NQ = NZ // 2
TOK = 128
SLOTS = 256
TERMS = 128
CUT = 384
WIDE = COLS + TERMS
WCUT = 768
F32 = jnp.float32
BF16 = jnp.bfloat16
MESH = pl.DeviceIdType.MESH
ORDER = (
    (2, 0, 1), (2, 1, 1), (3, 1, 0, 0), (3, 1, 1, 0), (0, 0), (0, 1), (2, 0, 2), (2, 1, 2),
    (4, 1, 0, 0), (3, 2, 0, 0), (3, 2, 1, 0), (4, 1, 1, 7), (3, 1, 0, 3), (3, 1, 1, 3), (3, 1, 0, 1), (3, 1, 1, 1),
    (4, 1, 0, 1), (2, 0, 3), (2, 1, 3), (1, 0), (1, 1), (3, 3, 0, 0), (4, 1, 1, 6), (3, 2, 0, 3),
    (3, 2, 1, 3), (3, 2, 0, 1), (3, 2, 1, 1), (4, 1, 0, 2), (2, 0, 4), (2, 1, 4), (3, 1, 0, 2), (3, 1, 1, 2),
    (3, 3, 1, 3), (4, 1, 1, 5), (3, 3, 0, 1), (3, 2, 1, 2), (3, 2, 0, 2), (4, 1, 0, 3), (4, 1, 1, 4), (3, 3, 1, 2),
)


def iota(shape, dim):
    return lax.broadcasted_iota(jnp.int32, shape, dim)


def one_hot(mask):
    return jnp.where(mask, 1.0, 0.0).astype(BF16)


def picked(table, rows):
    return jnp.dot(table, rows, preferred_element_type=F32).astype(BF16)


def flat(rows):
    return rows.reshape(SLOTS, rows.shape[-1])


def tiles(rows):
    return rows.reshape(8, 32, rows.shape[-1])


class Links:
    def __init__(self):
        self.x, self.s, self.core = (lax.axis_index(n) for n in ("sec", "seq", "tp"))
        self.y, self.z = self.s % NY, self.s // NY
        self.half, self.q = self.z % 2, self.z // 2
        self.pending = []

    def at(self, x=None, y=None, z=None, core=None):
        zz = self.z if z is None else z
        yy = self.y if y is None else y
        return {
            "sec": self.x if x is None else x,
            "seq": zz * NY + yy,
            "tp": self.core if core is None else core,
        }

    def remote(self, src, dst, sems, dev):
        return pltpu.make_async_remote_copy(
            src_ref=src, dst_ref=dst, send_sem=sems[0], recv_sem=sems[1], device_id=dev, device_id_type=MESH
        )

    def send(self, src, dst, sems, dev):
        copy = self.remote(src, dst, sems, dev)
        copy.start()
        self.pending.append(copy)

    def arrived(self, dst, sems):
        self.remote(dst, dst, sems, self.at(core=1 - self.core)).wait_recv()

    def finish(self):
        for copy in self.pending:
            copy.wait_send()


def pair(sems, *index):
    return sems[0].at[index], sems[1].at[index]


def product_core(net, refs, sems):
    shard, gain, weights, scaled, raw, product, give, take, home, squares, hidden, hidden0, terms, states_out, terms_out = refs
    swap_sem, pa, pf, pb, a2, b2, r_sem, o_sem, own_sem = sems
    x, y, z, q, half = net.x, net.y, net.z, net.q, net.half
    zm = z + 1 - 2 * half
    mate = net.at(core=1)

    def rows(qq, yy):
        return pl.ds(pl.multiple_of(qq * COLS + yy * WROWS, 16), WROWS)

    def wa(qq, yy):
        return weights.at[rows(qq, yy), pl.ds(0, WCUT)]

    def wb(qq, yy):
        return weights.at[rows(qq, yy), pl.ds(WCUT, BOTH - WCUT)]

    def wa_part(qq, yy, way):
        return weights.at[rows(qq, yy), pl.ds(way * WCUT // 2, WCUT // 2)]

    def wb_part(qq, yy, way):
        return weights.at[rows(qq, yy), pl.ds(WCUT + way * (BOTH - WCUT) // 2, (BOTH - WCUT) // 2)]

    y_way = net.at(y=(y + 1) % NY), net.at(y=(y + NY - 1) % NY)
    z_way = net.at(z=(z + 2) % NZ), net.at(z=(z + NZ - 2) % NZ)

    def along_y(j):
        piece = wa((q + j) % NQ, y)
        for way in (0, 1):
            net.send(piece, piece, pair(a2, way, 1, j), y_way[way])

    def along_z(j):
        piece = wb(q, (y + j) % NY)
        for way in (0, 1):
            net.send(piece, piece, pair(b2, way, 1, j), z_way[way])

    own = pltpu.make_async_copy(shard, weights.at[rows(q, y), pl.ds(0, COLS)], own_sem.at[0])
    own.start()
    net.send(hidden, hidden0, pair(swap_sem, 0), mate)
    own.wait()
    net.arrived(weights.at[rows(q, y), pl.ds(COLS, COLS)], pair(swap_sem, 1))
    for way in (0, 1):
        net.send(wa(q, y), wa(q, y), pair(pa, way), z_way[way])
    for way in (0, 1):
        net.send(wb(q, y), wb(q, y), pair(pb, way, 1), y_way[way])
    along_y(0)
    along_z(0)

    met = []

    def first_a(way):
        qq = (q + 3 - 2 * way) % NQ
        net.arrived(wa(qq, y), pair(pa, way))
        part = wa_part(qq, y, way)
        net.send(part, part, pair(pf, way), z_way[way])
        along_y(3 - 2 * way)

    def far_a(way):
        net.arrived(wa_part((q + 2) % NQ, y, way), pair(pf, way))
        if "far" in met:
            along_y(2)
        met.append("far")

    def first_b(way, d):
        yy = (y + (d if way else NY - d)) % NY
        part = wb_part(q, yy, way)
        piece = part if d == 4 else wb(q, yy)
        net.arrived(piece, pair(pb, way, d))
        if d < 3:
            net.send(piece, piece, pair(pb, way, d + 1), y_way[way])
        elif d == 3:
            net.send(part, part, pair(pb, way, 4), y_way[way])
        if d < 4:
            along_z(d if way else NY - d)
        elif "half" in met:
            along_z(4)
        else:
            met.append("half")

    waiting = [(3, d, way, j) for d in (1, 2, 3) for way in (0, 1) for j in range(NQ)]
    waiting += [(3, 4, j // 2, j) for j in range(NQ)]
    waiting += [(4, 1, way, j) for way in (0, 1) for j in range(NY)]
    waiting += [(4, 2, j // 4, j) for j in range(NY)]

    def next_a(d, way, j):
        waiting.remove((3, d, way, j))
        piece = wa((q + j) % NQ, (y + (d if way else NY - d)) % NY)
        net.arrived(piece, pair(a2, way, d, j))
        if d < 3 or (d == 3 and j // 2 == way):
            net.send(piece, piece, pair(a2, way, d + 1, j), y_way[way])

    def next_b(d, way, j):
        waiting.remove((4, d, way, j))
        piece = wb((q + (d if way else NQ - d)) % NQ, (y + j) % NY)
        net.arrived(piece, pair(b2, way, d, j))
        if d == 1 and j // 4 == way:
            net.send(piece, piece, pair(b2, way, 2, j), z_way[way])

    hops = (first_a, far_a, first_b, next_a, next_b)
    for kind, *index in ORDER:
        hops[kind](*index)

    for n, xx in enumerate((x, (x + NX - 1) % NX, (x + 1) % NX, (x + 2) % NX)):
        for i in range(2):
            net.arrived(raw.at[xx, pl.ds(i * TOK, TOK), :], pair(r_sem, n, i))
        g = gain[:, pl.ds(pl.multiple_of((2 * xx + half) * COLS, 128), COLS)]
        scaled[:, pl.ds(pl.multiple_of(xx * COLS, 128), COLS)] = (raw[xx].astype(F32) * g).astype(BF16)
    net.arrived(terms, pair(o_sem, 5))
    terms_out[...] = terms[:2, :]
    net.arrived(squares.at[0], pair(o_sem, 0))
    net.arrived(squares.at[1], pair(o_sem, 1))
    rate = lax.rsqrt((squares[0] + squares[1])[0:1] * (1.0 / D) + 1e-6)
    scale = jnp.sum(jnp.where(iota((SLOTS, 1), 0) == iota((1, SLOTS), 1), rate, 0.0), axis=1, keepdims=True)
    away = pl.ds(pl.multiple_of((1 - half) * TOK, TOK), TOK)
    near = pl.ds(pl.multiple_of(half * TOK, TOK), TOK)

    def arrive(kind):
        for item in [w for w in waiting if w[0] == kind]:
            hops[kind](*item[1:])

    def refine(c, start, width, slot):
        cols, own_cols = pl.ds(c * COLS + start, width), pl.ds(start, width)
        part = jnp.dot(scaled[...], weights[:, cols], preferred_element_type=F32)
        kept = jnp.where(half == c, 1.0, 0.0)
        product[:, cols] = part * scale + raw[x, :, own_cols].astype(F32) * kept
        give[c, :, own_cols] = product[away, cols].astype(BF16)
        net.send(give.at[c, :, own_cols], take.at[:, own_cols], pair(o_sem, slot), net.at(z=zm, core=c))

    arrive(4)
    refine(1, WCUT - COLS, BOTH - WCUT, 3)
    arrive(3)
    refine(1, 0, WCUT - COLS, 6)
    refine(0, 0, 256, 2)
    refine(0, 256, 384, 7)
    net.send(product.at[near, pl.ds(COLS, COLS)], home, pair(o_sem, 4), mate)
    net.arrived(take.at[:, pl.ds(0, 256)], pair(o_sem, 2))
    net.arrived(take.at[:, pl.ds(256, 384)], pair(o_sem, 7))
    states_out[...] = (product[near, :COLS] + take[...].astype(F32)).astype(BF16)
    net.finish()


def token_core(net, refs, sems):
    (
        hidden, hidden0, shard, old_logp, ref_logp, lengths, group_of, rewards, weights,
        info_own, info_y, info_line, info_z, send1, r1a, r1b, s2a, s2b, r2a, r2b,
        full_rows, terms, squares_own, squares, take, home, raw, states_out, terms_out,
    ) = refs
    swap_sem, iy, iz, del_sem, x_sem, r_sem, o_sem, own_info = sems
    x, y, z, q, half, s = net.x, net.y, net.z, net.q, net.half, net.s
    zm = z + 1 - 2 * half
    mate = net.at(core=0)
    info, length, group, reward, opening = own_info

    for k in range(1, NY):
        net.send(info_own, info_y.at[k], pair(iy, k), net.at(y=(y + k) % NY))
    own_rows = pl.ds(pl.multiple_of(q * COLS + y * WROWS, 16), WROWS)
    net.send(shard, weights.at[own_rows, pl.ds(COLS, COLS)], pair(swap_sem, 1), mate)
    line = info
    for k in range(1, NY):
        net.arrived(info_y.at[k], pair(iy, k))
        line += info_y[k]
    info_line[...] = line
    for k in range(1, NZ):
        net.send(info_line, info_z.at[k], pair(iz, k), net.at(z=(z + k) % NZ))

    lane = iota((8, 128), 1)
    col = iota((1, SLOTS), 1)
    spot = jnp.full((1, SLOTS), -1, jnp.int32)
    for i in range(4):
        p = col - i * LMAX
        spot = jnp.where((p >= 0) & (p < length[i]), opening[i] + p, spot)
    row = iota((SLOTS, 1), 0)
    turned = ((row // 4 % 8) * 8 + row // 32) * 4 + row % 4
    ratio = ref_logp[...] - old_logp[...]
    penalty = jnp.exp(ratio) - ratio - 1.0
    pen_col = jnp.sum(jnp.where(row == col, penalty, 0.0), axis=1, keepdims=True)
    swap = one_hot(turned == col)
    net.arrived(hidden0, pair(swap_sem, 0))

    total = line
    for k in range(1, NZ):
        net.arrived(info_z.at[k], pair(iz, k))
        total += info_z[k]

    first = (jnp.sum(jnp.where(lane < s, total, 0.0)) * 0.125).astype(jnp.int32)
    table1 = one_hot((((turned - first) & (SLOTS - 1))) == spot)
    table2 = one_hot((((row - first) & (SLOTS - 1))) == spot)
    lanes1, lanes2 = pl.ds(0, CUT), pl.ds(CUT, WIDE - CUT)

    def route_y(n, src, dst, lanes):
        dst[:, y] = src[:, y, :, lanes]
        for k in (4, 3, 5, 2, 6, 1, 7):
            t = (y + k) % NY
            net.send(src.at[:, t, :, lanes], dst.at[:, y], pair(del_sem, n, k), net.at(y=t))

    def wait_y(n, dst):
        for k in range(1, NY):
            net.arrived(dst.at[:, (y + NY - k) % NY], pair(del_sem, n, k))

    def route_z(n, src, dst, lanes):
        dst[z] = src[half, pl.ds(2 * q, 2), :, lanes]
        for k in (4, 3, 5, 2, 6, 1, 7):
            t = (z + k) % NZ
            net.send(src.at[t % 2, pl.ds(2 * (t // 2), 2), :, lanes], dst.at[z], pair(del_sem, n, k), net.at(z=t))

    def wait_z(n, dst):
        for k in range(1, NZ):
            net.arrived(dst.at[(z + NZ - k) % NZ], pair(del_sem, n, k))

    send1[0, :, :, :CUT] = tiles(picked(table1, hidden0[:, :CUT]))
    send1[1, :, :, :CUT] = tiles(picked(table1, hidden[:, :CUT]))
    route_y(0, send1, r1a, lanes1)

    mean = total * (1.0 / GROUP)
    mean_square = pltpu.roll(mean, 96, 1)
    spread = jnp.maximum(jnp.sqrt(mean_square - mean * mean), 1.0)
    adv_col = jnp.zeros((SLOTS, 1), F32)
    for i in range(4):
        value = jnp.where(lane == 64 + group[i], (reward[i] - mean) / spread, 0.0)
        adv_col = jnp.where(row // LMAX == i, jnp.sum(value) * 0.125, adv_col)
    term_lane = iota((SLOTS, TERMS), 1)
    own_terms = jnp.where(term_lane == 0, adv_col, jnp.where(term_lane == 1, pen_col, 0.0)).astype(BF16)
    send1[0, :, :, CUT:COLS] = tiles(picked(table2, hidden0[:, CUT:]))
    send1[1, :, :, CUT:COLS] = tiles(picked(table2, hidden[:, CUT:]))
    moved = tiles(picked(table2, own_terms))
    send1[0, :, :, COLS:] = moved
    send1[1, :, :, COLS:] = moved
    route_z(1, send1, r1b, lanes2)

    counts = total.astype(BF16)
    sender = iota((128, SLOTS), 0)
    natural = iota((128, SLOTS), 1) // 4
    swapped = (natural % 8) * 8 + natural // 8
    w = iota((TOK, 1), 0)
    same = w % 4 == col % 4

    def bounds(order):
        low = jnp.dot(counts, one_hot(sender < order), preferred_element_type=F32)[0:1]
        high = jnp.dot(counts, one_hot(sender <= order), preferred_element_type=F32)[0:1]
        return low, high

    def pick_table(limits, e):
        packed = ((w // 4) * SLOTS + ((2 * q + e) * NY + y) * 4 + w % 4).astype(F32)
        return one_hot((limits[0] <= packed) & (packed < limits[1]) & same)

    limits1, limits2 = bounds(natural), bounds(swapped)
    pick1 = [pick_table(limits1, e) for e in range(2)]
    pick2 = [pick_table(limits2, e) for e in range(2)]

    whole = pl.ds(0, CUT)
    wait_y(0, r1a)
    for c in range(2):
        s2a[c] = tiles(picked(swap, flat(r1a[c])))
    route_z(2, s2a, r2a, whole)
    wait_z(1, r1b)
    for e in range(2):
        s2b[e] = tiles(picked(swap, flat(r1b[:, e])))
    route_y(3, s2b, r2b, whole)

    wait_z(2, r2a)
    for e in range(2):
        full_rows[x, e * TOK : (e + 1) * TOK, :CUT] = picked(pick1[e], flat(r2a[:, e]))
    wait_y(3, r2b)
    for e in range(2):
        full_rows[x, e * TOK : (e + 1) * TOK, CUT:] = picked(pick2[e], flat(r2b[e, :, :, : COLS - CUT]))

    x_up, x_dn = net.at(x=(x + 1) % NX), net.at(x=(x + NX - 1) % NX)
    x_l, x_r, x_f = (x + NX - 1) % NX, (x + 1) % NX, (x + 2) % NX

    def part(xx, i):
        return full_rows.at[xx, pl.ds(i * TOK, TOK), :]

    def over(xx, i, way, slot):
        net.send(part(xx, i), part(xx, i), pair(x_sem, way, slot), (x_up, x_dn)[way])

    def down(xx, n, i):
        net.send(part(xx, i), raw.at[xx, pl.ds(i * TOK, TOK), :], pair(r_sem, n, i), mate)

    over(x, 0, 0, 0)
    over(x, 1, 1, 1)
    over(x, 1, 0, 1)
    over(x, 0, 1, 0)
    down(x, 0, 0)
    down(x, 0, 1)
    chosen = jnp.where(half == 0, pick2[0].astype(F32), pick2[1].astype(F32)).astype(BF16)
    terms[...] = lax.dot_general(
        flat(r2b[half, :, :, COLS - CUT :]), chosen, (((0,), (1,)), ((), ())), preferred_element_type=F32
    ).astype(BF16)
    net.send(terms, terms, pair(o_sem, 5), mate)
    terms_out[...] = terms[:2, :]

    square = [jnp.zeros((2 * TOK, 128), F32)]

    def add_squares(xx):
        wide = full_rows[xx].astype(F32)
        for t in range(COLS // 128):
            tile = wide[:, t * 128 : (t + 1) * 128]
            square[0] += tile * tile

    add_squares(x)
    net.arrived(part(x_l, 0), pair(x_sem, 0, 0))
    over(x_l, 0, 0, 2)
    net.arrived(part(x_r, 1), pair(x_sem, 1, 1))
    over(x_r, 1, 1, 2)
    down(x_l, 1, 0)
    down(x_r, 2, 1)
    net.arrived(part(x_l, 1), pair(x_sem, 0, 1))
    down(x_l, 1, 1)
    net.arrived(part(x_r, 0), pair(x_sem, 1, 0))
    down(x_r, 2, 0)
    add_squares(x_l)
    add_squares(x_r)
    net.arrived(part(x_f, 0), pair(x_sem, 0, 2))
    down(x_f, 3, 0)
    net.arrived(part(x_f, 1), pair(x_sem, 1, 2))
    down(x_f, 3, 1)
    add_squares(x_f)
    squares_own[...] = lax.dot_general(
        jnp.ones((8, 128), F32), square[0], (((1,), (1,)), ((), ())),
        precision=lax.Precision.HIGHEST, preferred_element_type=F32,
    )
    net.send(squares_own, squares.at[0], pair(o_sem, 0), mate)
    net.send(squares_own, squares.at[1], pair(o_sem, 1), net.at(z=zm, core=0))

    net.arrived(home, pair(o_sem, 4))
    net.arrived(take.at[:, pl.ds(WCUT - COLS, BOTH - WCUT)], pair(o_sem, 3))
    net.arrived(take.at[:, pl.ds(0, WCUT - COLS)], pair(o_sem, 6))
    states_out[...] = (home[...] + take[...].astype(F32)).astype(BF16)
    net.finish()


SCRATCH = dict(
    info_own=((8, 128), F32),
    info_y=((NY, 8, 128), F32),
    info_line=((8, 128), F32),
    info_z=((NZ, 8, 128), F32),
    send1=((2, 8, 32, WIDE), BF16),
    r1a=((2, 8, 32, CUT), BF16),
    r1b=((8, 2, 32, CUT), BF16),
    s2a=((2, 8, 32, CUT), BF16),
    s2b=((2, 8, 32, CUT), BF16),
    r2a=((8, 2, 32, CUT), BF16),
    r2b=((2, 8, 32, CUT), BF16),
    full_rows=((NX, 2 * TOK, COLS), BF16),
    raw=((NX, 2 * TOK, COLS), BF16),
    terms=((TERMS, TOK), BF16),
    hidden0=((SLOTS, COLS), BF16),
    weights=((NQ * COLS, BOTH), BF16),
    scaled=((2 * TOK, NX * COLS), BF16),
    product=((2 * TOK, BOTH), F32),
    give=((2, TOK, COLS), BF16),
    take=((TOK, COLS), BF16),
    home=((TOK, COLS), F32),
    squares_own=((8, 2 * TOK), F32),
    squares=((2, 8, 2 * TOK), F32),
    hidden=((SLOTS, COLS), BF16),
    shard=((WROWS, COLS), BF16),
    gain=((1, D), F32),
    old_logp=((1, SLOTS), F32),
    ref_logp=((1, SLOTS), F32),
)
INPUTS = ["hidden", "shard", "gain", "old_logp", "ref_logp"]
SEMAPHORES = dict(
    swap=(2,),
    iy=(8,),
    iz=(8,),
    deliver=(4, 8),
    pa=(2,),
    pf=(2,),
    pb=(2, 5),
    a2=(2, 5, 4),
    b2=(2, 3, 8),
    x=(2, 3),
    r=(4, 2),
    o=(8,),
)


def kernel(*refs):
    inputs, (states_out, terms_out), rest = refs[:8], refs[8:10], refs[10:]
    v = dict(zip(SCRATCH, rest))
    sem_refs = rest[len(SCRATCH) :]
    m = {n: (sem_refs[2 * i], sem_refs[2 * i + 1]) for i, n in enumerate(SEMAPHORES)}
    own_sem, in_sem, *scalars = sem_refs[2 * len(SEMAPHORES) :]
    hidden, shard, gain, old_logp, ref_logp = (v[n] for n in INPUTS)
    lengths, group_of, rewards = scalars

    net = Links()
    y, z = net.y, net.z
    other = 1 - net.core
    barrier = pltpu.get_barrier_semaphore()
    partners = [net.at(y=(y + k) % NY) for k in range(1, NY)]
    partners += [net.at(z=(z + k) % NZ) for k in range(1, NZ)]
    partners += [net.at(x=(net.x + k) % NX) for k in range(1, NX)]
    partners += [net.at(core=other), net.at(z=z + 1 - 2 * net.half, core=other)]
    for dev in partners:
        pl.semaphore_signal(barrier, inc=1, device_id=dev, device_id_type=MESH)

    loads = []
    for i, dst in enumerate([hidden, shard, gain, old_logp, ref_logp, lengths, group_of, rewards]):
        loads.append(pltpu.make_async_copy(inputs[i], dst, in_sem.at[i]))
    for i in (5, 6, 7, 0, 1, 2, 3, 4):
        loads[i].start()
    for i in (5, 6, 7, 0, 1, 2, 3, 4):
        loads[i].wait()
    lane = iota((8, 128), 1)
    length = [lengths[i] for i in range(4)]
    group = [group_of[i] for i in range(4)]
    reward = [rewards[i].astype(F32) for i in range(4)]
    opening = [0 * length[0]]
    for i in range(3):
        opening.append(opening[-1] + length[i])
    info = jnp.where(lane == net.s, (opening[3] + length[3]).astype(F32), 0.0)
    for i in range(4):
        info += jnp.where(lane == 64 + group[i], reward[i], 0.0)
        info += jnp.where(lane == 96 + group[i], reward[i] * reward[i], 0.0)
    v["info_own"][...] = info
    pl.semaphore_wait(barrier, len(partners))

    @pl.when(net.core == 0)
    def _():
        product_core(
            Links(),
            (
                shard, gain, v["weights"], v["scaled"], v["raw"], v["product"], v["give"], v["take"], v["home"], v["squares"],
                hidden, v["hidden0"], v["terms"], states_out, terms_out,
            ),
            (m["swap"], m["pa"], m["pf"], m["pb"], m["a2"], m["b2"], m["r"], m["o"], own_sem),
        )

    @pl.when(net.core == 1)
    def _():
        names = (
            "info_own", "info_y", "info_line", "info_z", "send1", "r1a", "r1b", "s2a", "s2b", "r2a", "r2b",
            "full_rows", "terms", "squares_own", "squares", "take", "home", "raw",
        )
        token_core(
            Links(),
            (hidden, v["hidden0"], shard, old_logp, ref_logp, lengths, group_of, rewards, v["weights"])
            + tuple(v[n] for n in names)
            + (states_out, terms_out),
            (m["swap"], m["iy"], m["iz"], m["deliver"], m["x"], m["r"], m["o"], (info, length, group, reward, opening)),
        )


def handed_on(states, terms, states_out, terms_out):
    states_out[...] = states[...]
    terms_out[...] = terms[...]


def shards(hidden, projection, norm_gain, old_logp, ref_logp, lengths, group_of, rewards):
    dma = pltpu.SemaphoreType.DMA
    vmem = pl.BlockSpec(memory_space=pltpu.VMEM)
    anywhere = pl.BlockSpec(memory_space=pltpu.MemorySpace.HBM)
    pairs = []
    for shape in SEMAPHORES.values():
        pairs += [dma(shape), dma(shape)]
    states, terms = pl.pallas_call(
        kernel,
        out_shape=(
            jax.ShapeDtypeStruct((TOK, COLS), BF16),
            jax.ShapeDtypeStruct((2, TOK), BF16),
        ),
        in_specs=[anywhere] * 8,
        out_specs=(vmem, vmem),
        scratch_shapes=[pltpu.VMEM(*spec) for spec in SCRATCH.values()] + pairs
        + [dma((1,)), dma((8,))]
        + [pltpu.SMEM((4,), jnp.int32)] * 3,
        compiler_params=pltpu.CompilerParams(collective_id=0, has_side_effects=True),
    )(
        hidden,
        projection,
        norm_gain.reshape(1, D),
        old_logp.reshape(1, SLOTS),
        ref_logp.reshape(1, SLOTS),
        lengths,
        group_of,
        rewards,
    )
    states, terms = pl.pallas_call(
        handed_on,
        out_shape=(jax.ShapeDtypeStruct((TOK, COLS), BF16), jax.ShapeDtypeStruct((2, TOK), BF16)),
        in_specs=[vmem] * 2,
        out_specs=(vmem, vmem),
    )(states, terms)
    return states, terms.T


def solution(mesh):
    in_specs = (
        P("seq", ("sec", "tp")),
        P("seq", ("sec", "tp")),
        P(),
        P("seq"),
        P("seq"),
        P("seq"),
        P("seq"),
        P("seq"),
    )
    out_specs = (P("seq", ("sec", "tp")), P("seq", None))
    return jax.shard_map(shards, mesh=mesh, in_specs=in_specs, out_specs=out_specs, check_vma=False)
```
